32 devices in a mesh: dp: 4 (over x, core), tensor: 2 (over y), layer: 4 (over z).
Axes of the slice: x: 2, y: 2, z: 4, core: 2. Of those that a mesh axis runs over, the one named last changes fastest.
Arguments:
- saved_inputs: bfloat16 [4, 2048, 8192], P(None, 'dp', ('tensor', 'layer')), may hold values from -6 to 6
- output_grad: bfloat16 [2048, 8192], P('dp', ('tensor', 'layer')), may hold values from -4 to 4
- weights: bfloat16 [4, 8192, 2, 4, 1024], P(None, 'tensor', None, 'layer'), may hold values from -0.0625 to 0.0625
- proj_in: bfloat16 [4, 64, 8192], P(None, None, ('tensor', 'layer')), may hold values from -0.0625 to 0.0625
- proj_out: bfloat16 [4, 64, 8192], P(None, None, ('tensor', 'layer')), may hold values from -0.0625 to 0.0625
- query_grads: bfloat16 [4, 1024, 4096], P('layer', ('dp', 'tensor')), may hold values from -0.00390625 to 0.00390625
- owner_map: int32 [4], replicated, may hold values from 0 to 3, each once
Outputs:
- input_grad: bfloat16 [2048, 8192], P('dp', ('tensor', 'layer'))
- scores: float32 [4, 1024], P('layer', ('dp', 'tensor'))
The draws below stay inside these ranges and needn't reach their ends.
Inputs may be any that keep to these rules, and one draw needn't show every extreme that they name: `owner_map`: each owner is named by exactly one layer.
All inputs are finite; a program needn't handle non-finite values.
Results may differ from the reference program's by a relative error of at most 0.035.
Values may be sent and summed in bfloat16 or wider, within the bound.
A program may use at most 256 MiB of HBM per device.

```python
import jax
import jax.numpy as jnp
from jax import lax

D = 8192
RANK = 64
LEN = 512
LAYERS = 4
TOKENS = 2048
NTRAIN = 4
NQ = 1024
N_TENSOR = 2
N_LAYER = 4


def levels(rng, extent, split, low, largest):
    def one(dim, shards_of):
        steps = jax.random.uniform(jax.random.fold_in(jax.random.fold_in(rng, 6), dim), (shards_of,), jnp.float32, low / len(split), largest / len(split))
        return jnp.repeat(jnp.exp(steps), extent[dim] // shards_of).reshape((-1,) + (1,) * (len(extent) - dim - 1))

    loudness = one(*split[0])
    for cut in split[1:]:
        loudness = loudness * one(*cut)
    return loudness


def scatter_about(key, shape, deviation, reach, shards=(), dtype=jnp.bfloat16):
    factor_of = levels(key, shape, shards, -0.22, 0.18) if shards else 1.0
    entries = jax.random.normal(key, shape, jnp.float32) * deviation * factor_of
    return jnp.minimum(jnp.maximum(entries, -reach), reach).astype(dtype)


def setup_inputs(seed: int = 0) -> dict:
    keys = jax.random.split(jax.random.key(seed), 8)
    return {
        "saved_inputs": scatter_about(keys[0], (LAYERS, TOKENS, D), 1.0, 6.0, ((1, 4), (2, 8))),
        "output_grad": scatter_about(keys[1], (TOKENS, D), 0.5, 4.0, ((0, 4), (1, 8))),
        "weights": scatter_about(keys[2], (LAYERS, D, N_TENSOR, N_LAYER, D // (N_TENSOR * N_LAYER)), D ** -0.5, 0.0625, ((1, 2), (3, 4))),
        "proj_in": scatter_about(keys[3], (LAYERS, RANK, D), D ** -0.5, 0.0625, ((2, 8),)),
        "proj_out": scatter_about(keys[4], (LAYERS, RANK, D), D ** -0.5, 0.0625, ((2, 8),)),
        "query_grads": scatter_about(keys[5], (LAYERS, NQ, RANK * RANK), (RANK * RANK * LEN) ** -0.5, 0.00390625, ((0, 4), (1, 8))),
        "owner_map": jax.random.permutation(keys[6], LAYERS).astype(jnp.int32),
    }


def reference(saved_inputs, output_grad, weights, proj_in, proj_out, query_grads, owner_map):
    layers = weights.shape[0]
    width = D // (N_TENSOR * N_LAYER)
    grad_now = output_grad.astype(jnp.float32)
    grad_bf = output_grad
    factors = [None] * layers
    for level in reversed(range(layers)):
        out_factor = jnp.dot(grad_bf, proj_out[level].T, preferred_element_type=jnp.float32)
        in_factor = jnp.dot(saved_inputs[level], proj_in[level].T, preferred_element_type=jnp.float32)
        factors[level] = (out_factor, in_factor)
        grid_grad = grad_bf.reshape(TOKENS, N_TENSOR, N_LAYER, width)
        summed = jnp.zeros((TOKENS, D), jnp.float32)
        for group in range(N_LAYER):
            columns = grid_grad[:, :, group, :].reshape(TOKENS, N_TENSOR * width)
            weight_cols = weights[level][:, :, group, :].reshape(D, N_TENSOR * width)
            term = lax.dot_general(columns, weight_cols, (((1,), (1,)), ((), ())), preferred_element_type=jnp.float32)
            rounded = lax.optimization_barrier(term.astype(jnp.bfloat16))
            summed = summed + rounded.astype(jnp.float32)
        grad_now = grad_now + summed
        grad_bf = grad_now.astype(jnp.bfloat16)
    scores = jnp.zeros((NTRAIN, NQ), jnp.float32)
    for level in range(layers):
        out_factor, in_factor = factors[level]
        left = out_factor.reshape(NTRAIN, LEN, RANK)
        right = in_factor.reshape(NTRAIN, LEN, RANK)
        blocks = jnp.einsum("eta,etb->eab", left, right, precision=lax.Precision.HIGHEST)
        blocks = blocks.reshape(NTRAIN, RANK * RANK).astype(jnp.bfloat16)
        queries = lax.dynamic_index_in_dim(query_grads, owner_map[level].astype(jnp.int32), 0, keepdims=False)
        scores = scores + lax.dot_general(blocks, queries, (((1,), (1,)), ((), ())), preferred_element_type=jnp.float32)
    return grad_bf, scores
```

```python
import functools

import jax
import jax.numpy as jnp
from jax import lax
from jax.experimental import pallas as pl
from jax.experimental.pallas import tpu as pltpu
from jax.sharding import PartitionSpec as P

LEN = 512
CHUNKS = 4
RAW = 3
MESH = pl.DeviceIdType.MESH
VMEM_BYTES = 67_000_000
NT = (((1,), (1,)), ((), ()))
NN = (((1,), (0,)), ((), ()))


def stack_kernel(
    dims,
    owner_ref,
    grad_hbm,
    weight_hbm,
    saved_hbm,
    proj_in_hbm,
    proj_out_hbm,
    query_hbm,
    out_hbm,
    score_ref,
    raw,
    flat,
    feats,
    part,
    from_left,
    from_right,
    total,
    proj_in,
    proj_out,
    queries,
    saved,
    out_factor,
    in_mine,
    in_peer,
    in_sum,
    run_send,
    run_recv,
    in_total,
    block,
    level_blocks,
    owner_send,
    owner_recv,
    tensor_send,
    tensor_recv,
    seq_blocks,
    score_send,
    score_recv,
    raw_sem,
    io_sem,
    load_sem,
    feat_send,
    feat_recv,
    part_send,
    left_recv,
    right_recv,
    in_send_sem,
    in_recv_sem,
    run_send_sem,
    run_recv_sem,
    gather_send_sem,
    gather_recv_sem,
    owner_send_sem,
    owner_recv_sem,
    tensor_send_sem,
    tensor_recv_sem,
    seq_send_sem,
    seq_recv_sem,
    score_send_sem,
    score_recv_sem,
):
    layers, n_layer, n_tensor, n_dp, rows, width, rank, step = dims
    last = n_layer - 1
    f32, bf16 = jnp.float32, jnp.bfloat16
    piece_rows = flat.shape[2]
    blocks = piece_rows // step
    per_level = n_layer * blocks
    n_tile = min(512, piece_rows)
    tokens = rows * CHUNKS
    share = tokens // n_tensor
    lanes = 2 * rank
    z = lax.axis_index("layer")
    t = lax.axis_index("tensor")
    d = lax.axis_index("dp")

    def nth_piece(i):
        return jnp.where(2 * z < n_layer, last - i, i)

    def raw_copy(n):
        level = layers - 1 - n // per_level
        i = (n // blocks) % n_layer
        start = pl.multiple_of(nth_piece(i) * piece_rows + (n % blocks) * step, step)
        return pltpu.make_async_copy(
            weight_hbm.at[level, pl.ds(start, step)], raw.at[n % RAW], raw_sem.at[n % RAW]
        )

    def relay(first, count):
        @pl.loop(first, first + count)
        def _(n):
            raw_copy(n).wait()

            @pl.when(n + RAW - 1 < layers * per_level)
            def _():
                raw_copy(n + RAW - 1).start()

            level = layers - 1 - n // per_level
            q = nth_piece((n // blocks) % n_layer)
            at = pl.ds(pl.multiple_of((n % blocks) * step, step), step)
            for a in range(n_tensor):
                flat[level % 2, q, at, a * width : (a + 1) * width] = raw[n % RAW, :, a, :]

    def feat_copy(level, c, shift):
        return pltpu.make_async_remote_copy(
            src_ref=feats.at[level % 2, c, t],
            dst_ref=feats.at[level % 2, c, t],
            send_sem=feat_send.at[level % 2, c, shift - 1],
            recv_sem=feat_recv.at[level % 2, c, shift - 1],
            device_id={"tensor": lax.rem(t + shift, n_tensor)},
            device_id_type=MESH,
        )

    def right_copy(slot, level, c, q):
        return pltpu.make_async_remote_copy(
            src_ref=part.at[slot, q],
            dst_ref=from_left.at[level % 2, c, last - q],
            send_sem=part_send.at[slot, q],
            recv_sem=left_recv.at[level % 2, c, last - q],
            device_id={"layer": z + 1},
            device_id_type=MESH,
        )

    def left_copy(slot, level, c, q):
        return pltpu.make_async_remote_copy(
            src_ref=part.at[slot, q],
            dst_ref=from_right.at[level % 2, c, q],
            send_sem=part_send.at[slot, q],
            recv_sem=right_recv.at[level % 2, c, q],
            device_id={"layer": z - 1},
            device_id_type=MESH,
        )

    def wait_part_sends(slot):
        for q in range(n_layer):

            if q > 0:

                @pl.when(q > z)
                def _():
                    right_copy(slot, 0, 0, q).wait_send()

            if q < last:

                @pl.when(q < z)
                def _():
                    left_copy(slot, 0, 0, q).wait_send()

    def multiply(slot, level, c, i):
        q = nth_piece(i)

        @pl.loop(0, piece_rows // n_tile)
        def _(j):
            at = pl.ds(pl.multiple_of(j * n_tile, n_tile), n_tile)
            acc = None
            for a in range(n_tensor):
                term = lax.dot_general(
                    feats[level % 2, c, a],
                    flat[level % 2, q, at, a * width : (a + 1) * width],
                    NT,
                    preferred_element_type=f32,
                )
                acc = term if acc is None else acc + term
            part[slot, q, :, at] = acc.astype(bf16)

        @pl.when((z == 0) & (q > 0))
        def _():
            right_copy(slot, level, c, q).start()

        @pl.when((z == last) & (q < last))
        def _():
            left_copy(slot, level, c, q).start()

    def forward(slot, level, c, s):
        right_piece, left_piece = last - s + z, s - last + z

        @pl.when((z > 0) & (right_piece <= last))
        def _():
            right_copy(slot, level, c, right_piece).wait_recv()

            @pl.when(right_piece > z)
            def _():
                part[slot, right_piece] = (
                    part[slot, right_piece].astype(f32)
                    + from_left[level % 2, c, last - right_piece].astype(f32)
                ).astype(bf16)
                right_copy(slot, level, c, right_piece).start()

        @pl.when((z < last) & (left_piece >= 0))
        def _():
            left_copy(slot, level, c, left_piece).wait_recv()

            @pl.when(left_piece < z)
            def _():
                part[slot, left_piece] = (
                    part[slot, left_piece].astype(f32)
                    + from_right[level % 2, c, left_piece].astype(f32)
                ).astype(bf16)
                left_copy(slot, level, c, left_piece).start()

    def grad_copy(c):
        return pltpu.make_async_copy(
            grad_hbm.at[pl.ds(c * rows, rows)], feats.at[(layers - 1) % 2, c, t], io_sem.at[c]
        )

    def out_copy(c):
        return pltpu.make_async_copy(
            feats.at[1, c, t], out_hbm.at[pl.ds(c * rows, rows)], io_sem.at[c]
        )

    def project(level, c):
        out_factor[level, c] = lax.dot_general(
            proj_out[level], feats[level % 2, c, t], NT, preferred_element_type=f32
        )

    def finish(slot, level, c):
        for shift in range(1, n_tensor):
            feat_copy(level, c, shift).wait_send()
        total[c] = total[c] + part[slot, z].astype(f32)

        @pl.when(z > 0)
        def _():
            total[c] = total[c] + from_left[level % 2, c, last - z].astype(f32)

        @pl.when(z < last)
        def _():
            total[c] = total[c] + from_right[level % 2, c, z].astype(f32)

        feats[(level + 1) % 2, c, t] = total[c].astype(bf16)

        @pl.when(level > 0)
        def _():
            for shift in range(1, n_tensor):
                feat_copy(level - 1, c, shift).start()
            project(jnp.maximum(level - 1, 0), c)

        @pl.when(level == 0)
        def _():
            out_copy(c).start()

    def saved_copy(level):
        return pltpu.make_async_copy(saved_hbm.at[level], saved, load_sem.at[3])

    def share_of(i):
        return pl.ds(pl.multiple_of(i * share, share), share)

    def in_copy(shift):
        peer = lax.rem(t + shift, n_tensor)
        return pltpu.make_async_remote_copy(
            src_ref=in_mine.at[:, share_of(peer)],
            dst_ref=in_peer.at[shift - 1],
            send_sem=in_send_sem.at[shift - 1],
            recv_sem=in_recv_sem.at[shift - 1],
            device_id={"tensor": peer},
            device_id_type=MESH,
        )

    def run_copy(side):
        return pltpu.make_async_remote_copy(
            src_ref=run_send.at[side],
            dst_ref=run_recv.at[side],
            send_sem=run_send_sem.at[side],
            recv_sem=run_recv_sem.at[side],
            device_id={"layer": z + (1 if side == 0 else -1)},
            device_id_type=MESH,
        )

    def gather_copy(shift):
        return pltpu.make_async_remote_copy(
            src_ref=in_total.at[:, share_of(t)],
            dst_ref=in_total.at[:, share_of(t)],
            send_sem=gather_send_sem.at[shift - 1],
            recv_sem=gather_recv_sem.at[shift - 1],
            device_id={"tensor": lax.rem(t + shift, n_tensor)},
            device_id_type=MESH,
        )

    def owner_copy(shift):
        peer = lax.rem(z + shift, n_layer)
        return pltpu.make_async_remote_copy(
            src_ref=owner_send.at[peer],
            dst_ref=owner_recv.at[shift - 1],
            send_sem=owner_send_sem.at[shift - 1],
            recv_sem=owner_recv_sem.at[shift - 1],
            device_id={"layer": peer},
            device_id_type=MESH,
        )

    def tensor_copy(shift):
        return pltpu.make_async_remote_copy(
            src_ref=tensor_send,
            dst_ref=tensor_recv.at[shift - 1],
            send_sem=tensor_send_sem.at[shift - 1],
            recv_sem=tensor_recv_sem.at[shift - 1],
            device_id={"tensor": lax.rem(t + shift, n_tensor)},
            device_id_type=MESH,
        )

    def seq_copy(shift):
        return pltpu.make_async_remote_copy(
            src_ref=seq_blocks.at[0],
            dst_ref=seq_blocks.at[shift],
            send_sem=seq_send_sem.at[shift - 1],
            recv_sem=seq_recv_sem.at[shift - 1],
            device_id={"dp": lax.rem(d + shift, n_dp)},
            device_id_type=MESH,
        )

    def score_copy(shift):
        peer = lax.rem(z + shift, n_layer)
        return pltpu.make_async_remote_copy(
            src_ref=score_send.at[lax.rem(d - peer + n_dp, n_dp)],
            dst_ref=score_recv.at[shift - 1],
            send_sem=score_send_sem.at[shift - 1],
            recv_sem=score_recv_sem.at[shift - 1],
            device_id={"layer": peer},
            device_id_type=MESH,
        )

    def project_saved(level):
        saved_copy(level).wait()
        pair, half = level // 2, level % 2
        value = lax.dot_general(saved[...], proj_in[pair], NT, preferred_element_type=f32)
        if half == 0:
            in_mine[pair] = value.astype(bf16)
        else:
            lane = lax.broadcasted_iota(jnp.int32, value.shape, 1)
            in_mine[pair] = jnp.where(lane < rank, in_mine[pair].astype(f32), value).astype(bf16)
        if level + 1 < layers:
            saved_copy(level + 1).start()
        else:
            for shift in range(1, n_tensor):
                in_copy(shift).start()

    def run_step(s):
        if s == 0:
            value = in_mine[:, share_of(t)].astype(f32)
            for shift in range(1, n_tensor):
                in_copy(shift).wait()
                value = value + in_peer[shift - 1].astype(f32)
            in_sum[...] = value
        if s < last:

            @pl.when(z == s)
            def _():
                if s > 0:
                    run_copy(0).wait_recv()
                    run_send[0] = (in_sum[...] + run_recv[0].astype(f32)).astype(bf16)
                else:
                    run_send[0] = in_sum[...].astype(bf16)
                run_copy(0).start()

            @pl.when(z == last - s)
            def _():
                if s > 0:
                    run_copy(1).wait_recv()
                    run_send[1] = (in_sum[...] + run_recv[1].astype(f32)).astype(bf16)
                else:
                    run_send[1] = in_sum[...].astype(bf16)
                run_copy(1).start()

        else:

            @pl.when(z == last)
            def _():
                run_copy(0).wait_recv()

            @pl.when(z == 0)
            def _():
                run_copy(1).wait_recv()

            @pl.when(z < last)
            def _():
                run_copy(0).wait_send()
                in_sum[...] = in_sum[...] + run_recv[1].astype(f32)

            @pl.when(z > 0)
            def _():
                run_copy(1).wait_send()
                in_sum[...] = in_sum[...] + run_recv[0].astype(f32)

            in_total[:, share_of(t)] = in_sum[...].astype(bf16)
            for shift in range(1, n_tensor):
                gather_copy(shift).start()

    def send_blocks():
        for shift in range(1, n_tensor):
            gather_copy(shift).wait()
        lane = lax.broadcasted_iota(jnp.int32, (rank // 2, lanes), 1)
        for level in range(layers):
            pair, half = level // 2, level % 2
            acc = None
            for c in range(CHUNKS):
                term = lax.dot_general(
                    out_factor[level, c],
                    in_total[pair, c * rows : (c + 1) * rows].astype(f32),
                    NN,
                    precision=lax.Precision.HIGHEST,
                    preferred_element_type=f32,
                )
                acc = term if acc is None else acc + term
            block[...] = acc
            even = block[pl.ds(0, rank // 2, stride=2), :]
            odd = block[pl.ds(1, rank // 2, stride=2), :]
            if half == 0:
                odd = pltpu.roll(odd, rank, 1)
            else:
                even = pltpu.roll(even, rank, 1)
            level_blocks[level] = jnp.where(lane < rank, even, odd)
        for q in range(n_layer):
            level = jnp.int32(0)
            for k in range(1, layers):
                level = jnp.where(owner_ref[k] == q, k, level)
            owner_send[q] = level_blocks[level]
        for shift in range(1, n_layer):
            owner_copy(shift).start()

    def sum_layers():
        value = owner_send[z]
        for shift in range(1, n_layer):
            owner_copy(shift).wait()
            value = value + owner_recv[shift - 1]
        tensor_send[...] = value
        for shift in range(1, n_tensor):
            tensor_copy(shift).start()

    def sum_tensor():
        value = tensor_send[...]
        for shift in range(1, n_tensor):
            tensor_copy(shift).wait()
            value = value + tensor_recv[shift - 1]
        seq_blocks[0] = value
        for shift in range(1, n_dp):
            seq_copy(shift).start()

    def score():
        for shift in range(1, n_dp):
            seq_copy(shift).wait()
        pltpu.make_async_copy(query_hbm, queries, load_sem.at[2]).wait()
        acc = None
        for j in range(rank // 2):
            term = lax.dot_general(
                seq_blocks[:, j, :].astype(bf16),
                queries[:, j * lanes : (j + 1) * lanes],
                NT,
                preferred_element_type=f32,
            )
            acc = term if acc is None else acc + term
        for k in range(n_dp):
            score_send[k] = acc[k : k + 1]
        for shift in range(1, n_layer):
            score_copy(shift).start()

    def sum_scores():
        value = score_send[lax.rem(d - z + n_dp, n_dp)]
        for shift in range(1, n_layer):
            score_copy(shift).wait()
            value = value + score_recv[shift - 1]
        score_ref[...] = value

    barrier = pltpu.get_barrier_semaphore()
    for axis, size, here in (("tensor", n_tensor, t), ("layer", n_layer, z), ("dp", n_dp, d)):
        for shift in range(1, size):
            pl.semaphore_signal(
                barrier, inc=1, device_id={axis: lax.rem(here + shift, size)}, device_id_type=MESH
            )

    for c in range(CHUNKS):
        grad_copy(c).start()
    for n in range(RAW - 1):
        raw_copy(n).start()
    pltpu.make_async_copy(proj_out_hbm, proj_out, load_sem.at[0]).start()
    pltpu.make_async_copy(proj_in_hbm, proj_in, load_sem.at[1]).start()
    pl.semaphore_wait(barrier, n_tensor + n_layer + n_dp - 3)

    for c in range(CHUNKS):
        grad_copy(c).wait()
        for shift in range(1, n_tensor):
            feat_copy(layers - 1, c, shift).start()

    phases = layers * CHUNKS
    fraction = per_level // (2 * CHUNKS)

    @pl.loop(0, phases + 1)
    def _(p):
        level = layers - 1 - p // CHUNKS
        c = p % CHUNKS
        slot = p % 2
        old_level = layers - 1 - (p - 1) // CHUNKS
        old_c = (p + CHUNKS - 1) % CHUNKS
        old_slot = (p + 1) % 2

        def at_phase(k, task, *args):
            @pl.when(p == k)
            def _():
                task(*args)

        @pl.when(p > 0)
        def _():
            forward(old_slot, old_level, old_c, 1)

        @pl.when(p < phases)
        def _():
            @pl.when(p >= 2)
            def _():
                wait_part_sends(slot)

            @pl.loop(0, n_layer)
            def _(i):
                @pl.when(p == 0)
                def _():
                    relay(i * blocks, blocks)

                @pl.when(i == 0)
                def _():
                    for shift in range(1, n_tensor):
                        feat_copy(level, c, shift).wait_recv()

                multiply(slot, level, c, i)

        base = (layers - level) * per_level + c * 2 * fraction
        count = jnp.where(p == 1, 2 * fraction, fraction)

        @pl.when(p == 0)
        def _():
            pltpu.make_async_copy(proj_out_hbm, proj_out, load_sem.at[0]).wait()
            pltpu.make_async_copy(proj_in_hbm, proj_in, load_sem.at[1]).wait()
            pltpu.make_async_copy(query_hbm, queries, load_sem.at[2]).start()
            saved_copy(0).start()
            for k in range(CHUNKS):
                total[k] = feats[(layers - 1) % 2, k, t].astype(f32)
                project(layers - 1, k)

        at_phase(phases - 3, send_blocks)
        at_phase(phases - 1, sum_tensor)

        @pl.when((p > 0) & (level > 0) & (p < phases))
        def _():
            relay(jnp.where(p == 1, per_level, base), count)

        for s in range(2, n_layer - 1):

            @pl.when(p > 0)
            def _():
                forward(old_slot, old_level, old_c, s)

        for k in range(layers):
            at_phase(CHUNKS + k, project_saved, k)
        for k in range(n_layer):
            at_phase(CHUNKS + layers + k, run_step, k)
        at_phase(phases - 2, sum_layers)
        at_phase(phases - 1, score)

        @pl.when((p > 0) & (level > 0) & (p < phases))
        def _():
            relay(base + 2 * fraction - count, count)

        @pl.when(p > 0)
        def _():
            forward(old_slot, old_level, old_c, last)
            finish(old_slot, old_level, old_c)

    wait_part_sends((phases - 2) % 2)
    wait_part_sends((phases - 1) % 2)
    sum_scores()
    for c in range(CHUNKS):
        out_copy(c).wait()


def on_device(saved_inputs, output_grad, weights, proj_in, proj_out, query_grads, owner_map):
    weights = weights[:, :, :, 0, :]
    layers, in_rows, n_tensor, width = weights.shape
    tokens = output_grad.shape[0]
    rank = proj_out.shape[1]
    n_queries = query_grads.shape[1]
    n_layer, n_dp = lax.axis_size("layer"), lax.axis_size("dp")
    assert tokens == LEN and n_dp == n_layer == layers and layers % 2 == 0
    rows = tokens // CHUNKS
    piece_rows = in_rows // n_layer
    step = min(256, piece_rows // 2)
    pairs, lanes, share = layers // 2, 2 * rank, tokens // n_tensor
    bf16, f32 = jnp.bfloat16, jnp.float32
    dma = pltpu.SemaphoreType.DMA
    hops = n_layer - 1
    anywhere = pl.BlockSpec(memory_space=pl.ANY)
    return pl.pallas_call(
        functools.partial(
            stack_kernel, (layers, n_layer, n_tensor, n_dp, rows, width, rank, step)
        ),
        out_shape=(
            jax.ShapeDtypeStruct((tokens, width), bf16),
            jax.ShapeDtypeStruct((1, n_queries), f32),
        ),
        in_specs=[pl.BlockSpec(memory_space=pltpu.SMEM)] + [anywhere] * 6,
        out_specs=(anywhere, pl.BlockSpec(memory_space=pltpu.VMEM)),
        scratch_shapes=[
            pltpu.VMEM((RAW, step, n_tensor, width), bf16),
            pltpu.VMEM((2, n_layer, piece_rows, n_tensor * width), bf16),
            pltpu.VMEM((2, CHUNKS, n_tensor, rows, width), bf16),
            pltpu.VMEM((2, n_layer, rows, piece_rows), bf16),
            pltpu.VMEM((2, CHUNKS, hops, rows, piece_rows), bf16),
            pltpu.VMEM((2, CHUNKS, hops, rows, piece_rows), bf16),
            pltpu.VMEM((CHUNKS, rows, width), f32),
            pltpu.VMEM((pairs, lanes, width), bf16),
            pltpu.VMEM((layers, rank, width), bf16),
            pltpu.VMEM(query_grads.shape[1:], bf16),
            pltpu.VMEM((tokens, width), bf16),
            pltpu.VMEM((layers, CHUNKS, rank, rows), f32),
            pltpu.VMEM((pairs, tokens, lanes), bf16),
            pltpu.VMEM((n_tensor - 1, pairs, share, lanes), bf16),
            pltpu.VMEM((pairs, share, lanes), f32),
            pltpu.VMEM((2, pairs, share, lanes), bf16),
            pltpu.VMEM((2, pairs, share, lanes), bf16),
            pltpu.VMEM((pairs, tokens, lanes), bf16),
            pltpu.VMEM((rank, lanes), f32),
            pltpu.VMEM((layers, rank // 2, lanes), f32),
            pltpu.VMEM((n_layer, rank // 2, lanes), f32),
            pltpu.VMEM((hops, rank // 2, lanes), f32),
            pltpu.VMEM((rank // 2, lanes), f32),
            pltpu.VMEM((n_tensor - 1, rank // 2, lanes), f32),
            pltpu.VMEM((n_dp, rank // 2, lanes), f32),
            pltpu.VMEM((n_dp, 1, n_queries), f32),
            pltpu.VMEM((hops, 1, n_queries), f32),
            dma((RAW,)),
            dma((CHUNKS,)),
            dma((4,)),
            dma((2, CHUNKS, n_tensor - 1)),
            dma((2, CHUNKS, n_tensor - 1)),
            dma((2, n_layer)),
            dma((2, CHUNKS, hops)),
            dma((2, CHUNKS, hops)),
            dma((n_tensor - 1,)),
            dma((n_tensor - 1,)),
            dma((2,)),
            dma((2,)),
            dma((n_tensor - 1,)),
            dma((n_tensor - 1,)),
            dma((hops,)),
            dma((hops,)),
            dma((n_tensor - 1,)),
            dma((n_tensor - 1,)),
            dma((n_dp - 1,)),
            dma((n_dp - 1,)),
            dma((hops,)),
            dma((hops,)),
        ],
        compiler_params=pltpu.CompilerParams(
            collective_id=0, has_side_effects=True, vmem_limit_bytes=VMEM_BYTES
        ),
        name="backward_stack",
    )(
        owner_map,
        output_grad,
        weights,
        saved_inputs,
        proj_in.reshape(pairs, lanes, width),
        proj_out,
        query_grads[0],
    )


def solution(mesh):
    in_specs = (
        P(None, "dp", ("tensor", "layer")),
        P("dp", ("tensor", "layer")),
        P(None, "tensor", None, "layer", None),
        P(None, None, ("tensor", "layer")),
        P(None, None, ("tensor", "layer")),
        P("layer", ("dp", "tensor"), None),
        P(),
    )
    out_specs = (P("dp", ("tensor", "layer")), P("layer", ("dp", "tensor")))
    return jax.shard_map(
        on_device, mesh=mesh, in_specs=in_specs, out_specs=out_specs, check_vma=False
    )
```

```python
import functools

import jax
import jax.numpy as jnp
from jax import lax
from jax.experimental import pallas as pl
from jax.experimental.pallas import tpu as pltpu
from jax.sharding import PartitionSpec as P

LEN = 512
CHUNKS = 4
RAW = 3
MESH = pl.DeviceIdType.MESH
VMEM_BYTES = 67_000_000
NT = (((1,), (1,)), ((), ()))
NN = (((1,), (0,)), ((), ()))


def stack_kernel(
    dims,
    owner_ref,
    grad_hbm,
    weight_hbm,
    saved_hbm,
    proj_in_hbm,
    proj_out_hbm,
    query_hbm,
    out_hbm,
    score_ref,
    raw,
    flat,
    feats,
    part,
    from_left,
    from_right,
    total,
    proj_in,
    proj_out,
    queries,
    saved,
    out_factor,
    in_mine,
    in_peer,
    in_sum,
    run_send,
    run_recv,
    in_total,
    block,
    level_blocks,
    owner_send,
    owner_recv,
    tensor_send,
    tensor_recv,
    seq_blocks,
    score_send,
    score_recv,
    raw_sem,
    io_sem,
    load_sem,
    feat_send,
    feat_recv,
    part_send,
    left_recv,
    right_recv,
    in_send_sem,
    in_recv_sem,
    run_send_sem,
    run_recv_sem,
    gather_send_sem,
    gather_recv_sem,
    owner_send_sem,
    owner_recv_sem,
    tensor_send_sem,
    tensor_recv_sem,
    seq_send_sem,
    seq_recv_sem,
    score_send_sem,
    score_recv_sem,
):
    layers, n_layer, n_tensor, n_dp, rows, width, rank, step = dims
    last = n_layer - 1
    f32, bf16 = jnp.float32, jnp.bfloat16
    piece_rows = flat.shape[2]
    blocks = piece_rows // step
    per_level = n_layer * blocks
    n_tile = min(512, piece_rows)
    tokens = rows * CHUNKS
    share = tokens // n_tensor
    lanes = 2 * rank
    z = lax.axis_index("layer")
    t = lax.axis_index("tensor")
    d = lax.axis_index("dp")

    def nth_piece(i):
        return jnp.where(2 * z < n_layer, last - i, i)

    def raw_copy(n):
        level = layers - 1 - n // per_level
        i = (n // blocks) % n_layer
        start = pl.multiple_of(nth_piece(i) * piece_rows + (n % blocks) * step, step)
        return pltpu.make_async_copy(
            weight_hbm.at[level, pl.ds(start, step)], raw.at[n % RAW], raw_sem.at[n % RAW]
        )

    def relay(first, count):
        @pl.loop(first, first + count)
        def _(n):
            raw_copy(n).wait()

            @pl.when(n + RAW - 1 < layers * per_level)
            def _():
                raw_copy(n + RAW - 1).start()

            level = layers - 1 - n // per_level
            q = nth_piece((n // blocks) % n_layer)
            at = pl.ds(pl.multiple_of((n % blocks) * step, step), step)
            by_feature = jnp.swapaxes(raw[n % RAW], 0, 1)
            for a in range(n_tensor):
                flat[level % 2, q, at, a * width : (a + 1) * width] = by_feature[a]

    def span(c, count=1):
        return pl.ds(pl.multiple_of(c * rows, rows), count * rows)

    def feat_copy(level, c, shift):
        return pltpu.make_async_remote_copy(
            src_ref=feats.at[level % 2, t, span(c)],
            dst_ref=feats.at[level % 2, t, span(c)],
            send_sem=feat_send.at[level % 2, c, shift - 1],
            recv_sem=feat_recv.at[level % 2, c, shift - 1],
            device_id={"tensor": lax.rem(t + shift, n_tensor)},
            device_id_type=MESH,
        )

    def right_copy(slot, level, c, q):
        return pltpu.make_async_remote_copy(
            src_ref=part.at[slot, q, span(c % 2)],
            dst_ref=from_left.at[level % 2, c, last - q],
            send_sem=part_send.at[slot, c % 2, q],
            recv_sem=left_recv.at[level % 2, c, last - q],
            device_id={"layer": z + 1},
            device_id_type=MESH,
        )

    def left_copy(slot, level, c, q):
        return pltpu.make_async_remote_copy(
            src_ref=part.at[slot, q, span(c % 2)],
            dst_ref=from_right.at[level % 2, c, q],
            send_sem=part_send.at[slot, c % 2, q],
            recv_sem=right_recv.at[level % 2, c, q],
            device_id={"layer": z - 1},
            device_id_type=MESH,
        )

    def wait_part_sends(slot, half):
        for q in range(n_layer):

            if q > 0:

                @pl.when(q > z)
                def _():
                    right_copy(slot, 0, half, q).wait_send()

            if q < last:

                @pl.when(q < z)
                def _():
                    left_copy(slot, 0, half, q).wait_send()

    def send_piece(slot, level, c, q):
        @pl.when((z == 0) & (q > 0))
        def _():
            right_copy(slot, level, c, q).start()

        @pl.when((z == last) & (q < last))
        def _():
            left_copy(slot, level, c, q).start()

    def multiply(slot, level, c, i, count):
        q = nth_piece(i)
        here, there = span(c, count), span(c % 2, count)

        @pl.loop(0, piece_rows // n_tile)
        def _(j):
            at = pl.ds(pl.multiple_of(j * n_tile, n_tile), n_tile)
            acc = None
            for a in range(n_tensor):
                term = lax.dot_general(
                    feats[level % 2, a, here, :],
                    flat[level % 2, q, at, a * width : (a + 1) * width],
                    NT,
                    preferred_element_type=f32,
                )
                acc = term if acc is None else acc + term
            part[slot, q, there, at] = acc.astype(bf16)

        send_piece(slot, level, c, q)

    def forward(slot, level, c, s):
        right_piece, left_piece = last - s + z, s - last + z

        @pl.when((z > 0) & (right_piece <= last))
        def _():
            right_copy(slot, level, c, right_piece).wait_recv()

            @pl.when(right_piece > z)
            def _():
                part[slot, right_piece, span(c % 2), :] = (
                    part[slot, right_piece, span(c % 2), :].astype(f32)
                    + from_left[level % 2, c, last - right_piece].astype(f32)
                ).astype(bf16)
                right_copy(slot, level, c, right_piece).start()

        @pl.when((z < last) & (left_piece >= 0))
        def _():
            left_copy(slot, level, c, left_piece).wait_recv()

            @pl.when(left_piece < z)
            def _():
                part[slot, left_piece, span(c % 2), :] = (
                    part[slot, left_piece, span(c % 2), :].astype(f32)
                    + from_right[level % 2, c, left_piece].astype(f32)
                ).astype(bf16)
                left_copy(slot, level, c, left_piece).start()

    def grad_copy(c):
        return pltpu.make_async_copy(
            grad_hbm.at[pl.ds(c * rows, rows)], feats.at[(layers - 1) % 2, t, span(c)], io_sem.at[c]
        )

    def out_copy(c):
        return pltpu.make_async_copy(
            feats.at[1, t, span(c)], out_hbm.at[pl.ds(c * rows, rows)], io_sem.at[c]
        )

    def project(level, c):
        out_factor[level, c] = lax.dot_general(
            proj_out[level], feats[level % 2, t, span(c), :], NT, preferred_element_type=f32
        )

    def finish(slot, level, c):
        for shift in range(1, n_tensor):
            feat_copy(level, c, shift).wait_send()
        total[c] = total[c] + part[slot, z, span(c % 2), :].astype(f32)

        @pl.when(z > 0)
        def _():
            total[c] = total[c] + from_left[level % 2, c, last - z].astype(f32)

        @pl.when(z < last)
        def _():
            total[c] = total[c] + from_right[level % 2, c, z].astype(f32)

        feats[(level + 1) % 2, t, span(c), :] = total[c].astype(bf16)

        @pl.when(level > 0)
        def _():
            for shift in range(1, n_tensor):
                feat_copy(level - 1, c, shift).start()
            project(jnp.maximum(level - 1, 0), c)

        @pl.when(level == 0)
        def _():
            out_copy(c).start()

    def saved_copy(level):
        return pltpu.make_async_copy(saved_hbm.at[level], saved, load_sem.at[3])

    def share_of(i):
        return pl.ds(pl.multiple_of(i * share, share), share)

    def in_copy(shift):
        peer = lax.rem(t + shift, n_tensor)
        return pltpu.make_async_remote_copy(
            src_ref=in_mine.at[:, share_of(peer)],
            dst_ref=in_peer.at[shift - 1],
            send_sem=in_send_sem.at[shift - 1],
            recv_sem=in_recv_sem.at[shift - 1],
            device_id={"tensor": peer},
            device_id_type=MESH,
        )

    def run_copy(side):
        return pltpu.make_async_remote_copy(
            src_ref=run_send.at[side],
            dst_ref=run_recv.at[side],
            send_sem=run_send_sem.at[side],
            recv_sem=run_recv_sem.at[side],
            device_id={"layer": z + (1 if side == 0 else -1)},
            device_id_type=MESH,
        )

    def gather_copy(shift):
        return pltpu.make_async_remote_copy(
            src_ref=in_total.at[:, share_of(t)],
            dst_ref=in_total.at[:, share_of(t)],
            send_sem=gather_send_sem.at[shift - 1],
            recv_sem=gather_recv_sem.at[shift - 1],
            device_id={"tensor": lax.rem(t + shift, n_tensor)},
            device_id_type=MESH,
        )

    def owner_copy(shift):
        peer = lax.rem(z + shift, n_layer)
        return pltpu.make_async_remote_copy(
            src_ref=owner_send.at[peer],
            dst_ref=owner_recv.at[shift - 1],
            send_sem=owner_send_sem.at[shift - 1],
            recv_sem=owner_recv_sem.at[shift - 1],
            device_id={"layer": peer},
            device_id_type=MESH,
        )

    def tensor_copy(shift):
        return pltpu.make_async_remote_copy(
            src_ref=tensor_send,
            dst_ref=tensor_recv.at[shift - 1],
            send_sem=tensor_send_sem.at[shift - 1],
            recv_sem=tensor_recv_sem.at[shift - 1],
            device_id={"tensor": lax.rem(t + shift, n_tensor)},
            device_id_type=MESH,
        )

    def seq_copy(shift):
        return pltpu.make_async_remote_copy(
            src_ref=seq_blocks.at[0],
            dst_ref=seq_blocks.at[shift],
            send_sem=seq_send_sem.at[shift - 1],
            recv_sem=seq_recv_sem.at[shift - 1],
            device_id={"dp": lax.rem(d + shift, n_dp)},
            device_id_type=MESH,
        )

    def score_copy(shift):
        peer = lax.rem(z + shift, n_layer)
        return pltpu.make_async_remote_copy(
            src_ref=score_send.at[lax.rem(d - peer + n_dp, n_dp)],
            dst_ref=score_recv.at[shift - 1],
            send_sem=score_send_sem.at[shift - 1],
            recv_sem=score_recv_sem.at[shift - 1],
            device_id={"layer": peer},
            device_id_type=MESH,
        )

    def project_saved(level):
        saved_copy(level).wait()
        pair, half = level // 2, level % 2
        value = lax.dot_general(saved[...], proj_in[pair], NT, preferred_element_type=f32)
        if half == 0:
            in_mine[pair] = value.astype(bf16)
        else:
            lane = lax.broadcasted_iota(jnp.int32, value.shape, 1)
            in_mine[pair] = jnp.where(lane < rank, in_mine[pair].astype(f32), value).astype(bf16)
        if level + 1 < layers:
            saved_copy(level + 1).start()
        else:
            for shift in range(1, n_tensor):
                in_copy(shift).start()

    def run_step(s):
        if s == 0:
            value = in_mine[:, share_of(t)].astype(f32)
            for shift in range(1, n_tensor):
                in_copy(shift).wait()
                value = value + in_peer[shift - 1].astype(f32)
            in_sum[...] = value
        if s < last:

            @pl.when(z == s)
            def _():
                if s > 0:
                    run_copy(0).wait_recv()
                    run_send[0] = (in_sum[...] + run_recv[0].astype(f32)).astype(bf16)
                else:
                    run_send[0] = in_sum[...].astype(bf16)
                run_copy(0).start()

            @pl.when(z == last - s)
            def _():
                if s > 0:
                    run_copy(1).wait_recv()
                    run_send[1] = (in_sum[...] + run_recv[1].astype(f32)).astype(bf16)
                else:
                    run_send[1] = in_sum[...].astype(bf16)
                run_copy(1).start()

        else:

            @pl.when(z == last)
            def _():
                run_copy(0).wait_recv()

            @pl.when(z == 0)
            def _():
                run_copy(1).wait_recv()

            @pl.when(z < last)
            def _():
                run_copy(0).wait_send()
                in_sum[...] = in_sum[...] + run_recv[1].astype(f32)

            @pl.when(z > 0)
            def _():
                run_copy(1).wait_send()
                in_sum[...] = in_sum[...] + run_recv[0].astype(f32)

            in_total[:, share_of(t)] = in_sum[...].astype(bf16)
            for shift in range(1, n_tensor):
                gather_copy(shift).start()

    def send_blocks():
        for shift in range(1, n_tensor):
            gather_copy(shift).wait()
        lane = lax.broadcasted_iota(jnp.int32, (rank // 2, lanes), 1)
        for level in range(layers):
            pair, half = level // 2, level % 2
            acc = None
            for c in range(CHUNKS):
                term = lax.dot_general(
                    out_factor[level, c],
                    in_total[pair, c * rows : (c + 1) * rows].astype(f32),
                    NN,
                    precision=lax.Precision.HIGHEST,
                    preferred_element_type=f32,
                )
                acc = term if acc is None else acc + term
            block[...] = acc
            even = block[pl.ds(0, rank // 2, stride=2), :]
            odd = block[pl.ds(1, rank // 2, stride=2), :]
            if half == 0:
                odd = pltpu.roll(odd, rank, 1)
            else:
                even = pltpu.roll(even, rank, 1)
            level_blocks[level] = jnp.where(lane < rank, even, odd)
        for q in range(n_layer):
            level = jnp.int32(0)
            for k in range(1, layers):
                level = jnp.where(owner_ref[k] == q, k, level)
            owner_send[q] = level_blocks[level]
        for shift in range(1, n_layer):
            owner_copy(shift).start()

    def sum_layers():
        value = owner_send[z]
        for shift in range(1, n_layer):
            owner_copy(shift).wait()
            value = value + owner_recv[shift - 1]
        tensor_send[...] = value
        for shift in range(1, n_tensor):
            tensor_copy(shift).start()

    def sum_tensor():
        value = tensor_send[...]
        for shift in range(1, n_tensor):
            tensor_copy(shift).wait()
            value = value + tensor_recv[shift - 1]
        seq_blocks[0] = value
        for shift in range(1, n_dp):
            seq_copy(shift).start()

    def score():
        for shift in range(1, n_dp):
            seq_copy(shift).wait()
        pltpu.make_async_copy(query_hbm, queries, load_sem.at[2]).wait()
        acc = None
        for j in range(rank // 2):
            term = lax.dot_general(
                seq_blocks[:, j, :].astype(bf16),
                queries[:, j * lanes : (j + 1) * lanes],
                NT,
                preferred_element_type=f32,
            )
            acc = term if acc is None else acc + term
        for k in range(n_dp):
            score_send[k] = acc[k : k + 1]
        for shift in range(1, n_layer):
            score_copy(shift).start()

    def sum_scores():
        value = score_send[lax.rem(d - z + n_dp, n_dp)]
        for shift in range(1, n_layer):
            score_copy(shift).wait()
            value = value + score_recv[shift - 1]
        score_ref[...] = value

    barrier = pltpu.get_barrier_semaphore()
    for axis, size, here in (("tensor", n_tensor, t), ("layer", n_layer, z), ("dp", n_dp, d)):
        for shift in range(1, size):
            pl.semaphore_signal(
                barrier, inc=1, device_id={axis: lax.rem(here + shift, size)}, device_id_type=MESH
            )

    for c in range(CHUNKS):
        grad_copy(c).start()
    for n in range(RAW - 1):
        raw_copy(n).start()
    pltpu.make_async_copy(proj_out_hbm, proj_out, load_sem.at[0]).start()
    pltpu.make_async_copy(proj_in_hbm, proj_in, load_sem.at[1]).start()
    pl.semaphore_wait(barrier, n_tensor + n_layer + n_dp - 3)

    for c in range(CHUNKS):
        grad_copy(c).wait()
        for shift in range(1, n_tensor):
            feat_copy(layers - 1, c, shift).start()

    phases = layers * CHUNKS
    fraction = per_level // (2 * CHUNKS)

    @pl.loop(0, phases + 1)
    def _(p):
        level = layers - 1 - p // CHUNKS
        c = p % CHUNKS
        slot = (p // 2) % 2
        old_level = layers - 1 - (p - 1) // CHUNKS
        old_c = (p + CHUNKS - 1) % CHUNKS
        old_slot = ((p - 1) // 2) % 2

        def at_phase(k, task, *args):
            @pl.when(p == k)
            def _():
                task(*args)

        @pl.when(p > 0)
        def _():
            forward(old_slot, old_level, old_c, 1)

        @pl.when(p < 2)
        def _():
            @pl.loop(0, n_layer)
            def _(i):
                @pl.when(p == 0)
                def _():
                    relay(i * blocks, blocks)

                @pl.when(i == 0)
                def _():
                    for shift in range(1, n_tensor):
                        feat_copy(level, c, shift).wait_recv()

                multiply(slot, level, c, i, 1)

        @pl.when((p >= 2) & (p < phases) & (c % 2 == 0))
        def _():
            @pl.when(p >= 4)
            def _():
                wait_part_sends(slot, 0)
                wait_part_sends(slot, 1)

            for shift in range(1, n_tensor):
                feat_copy(level, c, shift).wait_recv()
                feat_copy(level, c + 1, shift).wait_recv()

            @pl.loop(0, n_layer)
            def _(i):
                multiply(slot, level, c, i, 2)

            for i in range(n_layer):
                send_piece(slot, level, c + 1, nth_piece(i))

        base = (layers - level) * per_level + c * 2 * fraction
        early = jnp.where(p == 1, 2 * fraction, jnp.where(c % 2 == 1, fraction, 0))
        late = jnp.where((p == 1) | (c % 2 == 0), 2 * fraction, fraction)
        @pl.when(p == 0)
        def _():
            pltpu.make_async_copy(proj_out_hbm, proj_out, load_sem.at[0]).wait()
            pltpu.make_async_copy(proj_in_hbm, proj_in, load_sem.at[1]).wait()
            pltpu.make_async_copy(query_hbm, queries, load_sem.at[2]).start()
            saved_copy(0).start()
            for k in range(CHUNKS):
                total[k] = feats[(layers - 1) % 2, t, span(k), :].astype(f32)
                project(layers - 1, k)

        at_phase(phases - 3, send_blocks)
        at_phase(phases - 1, sum_tensor)

        @pl.when((p > 0) & (level > 0) & (p < phases))
        def _():
            relay(jnp.where(p == 1, per_level, base), early)

        for s in range(2, n_layer - 1):

            @pl.when(p > 0)
            def _():
                forward(old_slot, old_level, old_c, s)

        for k in range(layers):
            at_phase(CHUNKS + k, project_saved, k)
        for k in range(n_layer):
            at_phase(CHUNKS + layers + k, run_step, k)
        at_phase(phases - 2, sum_layers)
        at_phase(phases - 1, score)

        @pl.when((p > 0) & (level > 0) & (p < phases))
        def _():
            relay(base + 2 * fraction - late, late)

        @pl.when(p > 0)
        def _():
            forward(old_slot, old_level, old_c, last)
            finish(old_slot, old_level, old_c)

    for k in range(2):
        wait_part_sends(k, 0)
        wait_part_sends(k, 1)
    sum_scores()
    for c in range(CHUNKS):
        out_copy(c).wait()


def on_device(saved_inputs, output_grad, weights, proj_in, proj_out, query_grads, owner_map):
    weights = weights[:, :, :, 0, :]
    layers, in_rows, n_tensor, width = weights.shape
    tokens = output_grad.shape[0]
    rank = proj_out.shape[1]
    n_queries = query_grads.shape[1]
    n_layer, n_dp = lax.axis_size("layer"), lax.axis_size("dp")
    assert tokens == LEN and n_dp == n_layer == layers and layers % 2 == 0
    rows = tokens // CHUNKS
    piece_rows = in_rows // n_layer
    step = min(256, piece_rows // 2)
    pairs, lanes, share = layers // 2, 2 * rank, tokens // n_tensor
    bf16, f32 = jnp.bfloat16, jnp.float32
    dma = pltpu.SemaphoreType.DMA
    hops = n_layer - 1
    anywhere = pl.BlockSpec(memory_space=pl.ANY)
    return pl.pallas_call(
        functools.partial(
            stack_kernel, (layers, n_layer, n_tensor, n_dp, rows, width, rank, step)
        ),
        out_shape=(
            jax.ShapeDtypeStruct((tokens, width), bf16),
            jax.ShapeDtypeStruct((1, n_queries), f32),
        ),
        in_specs=[pl.BlockSpec(memory_space=pltpu.SMEM)] + [anywhere] * 6,
        out_specs=(anywhere, pl.BlockSpec(memory_space=pltpu.VMEM)),
        scratch_shapes=[
            pltpu.VMEM((RAW, step, n_tensor, width), bf16),
            pltpu.VMEM((2, n_layer, piece_rows, n_tensor * width), bf16),
            pltpu.VMEM((2, n_tensor, tokens, width), bf16),
            pltpu.VMEM((2, n_layer, 2 * rows, piece_rows), bf16),
            pltpu.VMEM((2, CHUNKS, hops, rows, piece_rows), bf16),
            pltpu.VMEM((2, CHUNKS, hops, rows, piece_rows), bf16),
            pltpu.VMEM((CHUNKS, rows, width), f32),
            pltpu.VMEM((pairs, lanes, width), bf16),
            pltpu.VMEM((layers, rank, width), bf16),
            pltpu.VMEM(query_grads.shape[1:], bf16),
            pltpu.VMEM((tokens, width), bf16),
            pltpu.VMEM((layers, CHUNKS, rank, rows), f32),
            pltpu.VMEM((pairs, tokens, lanes), bf16),
            pltpu.VMEM((n_tensor - 1, pairs, share, lanes), bf16),
            pltpu.VMEM((pairs, share, lanes), f32),
            pltpu.VMEM((2, pairs, share, lanes), bf16),
            pltpu.VMEM((2, pairs, share, lanes), bf16),
            pltpu.VMEM((pairs, tokens, lanes), bf16),
            pltpu.VMEM((rank, lanes), f32),
            pltpu.VMEM((layers, rank // 2, lanes), f32),
            pltpu.VMEM((n_layer, rank // 2, lanes), f32),
            pltpu.VMEM((hops, rank // 2, lanes), f32),
            pltpu.VMEM((rank // 2, lanes), f32),
            pltpu.VMEM((n_tensor - 1, rank // 2, lanes), f32),
            pltpu.VMEM((n_dp, rank // 2, lanes), f32),
            pltpu.VMEM((n_dp, 1, n_queries), f32),
            pltpu.VMEM((hops, 1, n_queries), f32),
            dma((RAW,)),
            dma((CHUNKS,)),
            dma((4,)),
            dma((2, CHUNKS, n_tensor - 1)),
            dma((2, CHUNKS, n_tensor - 1)),
            dma((2, 2, n_layer)),
            dma((2, CHUNKS, hops)),
            dma((2, CHUNKS, hops)),
            dma((n_tensor - 1,)),
            dma((n_tensor - 1,)),
            dma((2,)),
            dma((2,)),
            dma((n_tensor - 1,)),
            dma((n_tensor - 1,)),
            dma((hops,)),
            dma((hops,)),
            dma((n_tensor - 1,)),
            dma((n_tensor - 1,)),
            dma((n_dp - 1,)),
            dma((n_dp - 1,)),
            dma((hops,)),
            dma((hops,)),
        ],
        compiler_params=pltpu.CompilerParams(
            collective_id=0, has_side_effects=True, vmem_limit_bytes=VMEM_BYTES
        ),
        name="backward_stack",
    )(
        owner_map,
        output_grad,
        weights,
        saved_inputs,
        proj_in.reshape(pairs, lanes, width),
        proj_out,
        query_grads[0],
    )


def solution(mesh):
    in_specs = (
        P(None, "dp", ("tensor", "layer")),
        P("dp", ("tensor", "layer")),
        P(None, "tensor", None, "layer", None),
        P(None, None, ("tensor", "layer")),
        P(None, None, ("tensor", "layer")),
        P("layer", ("dp", "tensor"), None),
        P(),
    )
    out_specs = (P("dp", ("tensor", "layer")), P("layer", ("dp", "tensor")))
    return jax.shard_map(
        on_device, mesh=mesh, in_specs=in_specs, out_specs=out_specs, check_vma=False
    )
```

```python
import functools

import jax
import jax.numpy as jnp
from jax import lax
from jax.experimental import pallas as pl
from jax.experimental.pallas import tpu as pltpu
from jax.sharding import PartitionSpec as P

LEN = 512
CHUNKS = 4
RAW = 3
MESH = pl.DeviceIdType.MESH
VMEM_BYTES = 67_000_000
NT = (((1,), (1,)), ((), ()))
NN = (((1,), (0,)), ((), ()))


def stack_kernel(
    dims,
    owner_ref,
    grad_hbm,
    weight_hbm,
    saved_hbm,
    proj_in_hbm,
    proj_out_hbm,
    query_hbm,
    out_hbm,
    score_ref,
    raw,
    flat,
    feats,
    part,
    from_left,
    from_right,
    total,
    proj_in,
    proj_out,
    queries,
    saved,
    out_factor,
    in_mine,
    in_peer,
    in_sum,
    run_send,
    run_recv,
    in_total,
    block,
    level_blocks,
    owner_send,
    owner_recv,
    tensor_send,
    tensor_recv,
    seq_blocks,
    score_send,
    score_recv,
    raw_sem,
    io_sem,
    load_sem,
    feat_send,
    feat_recv,
    first_recv,
    part_send,
    left_recv,
    right_recv,
    in_send_sem,
    in_recv_sem,
    run_send_sem,
    run_recv_sem,
    gather_send_sem,
    gather_recv_sem,
    owner_send_sem,
    owner_recv_sem,
    tensor_send_sem,
    tensor_recv_sem,
    seq_send_sem,
    seq_recv_sem,
    score_send_sem,
    score_recv_sem,
):
    layers, n_layer, n_tensor, n_dp, rows, width, rank, step = dims
    last = n_layer - 1
    f32, bf16 = jnp.float32, jnp.bfloat16
    piece_rows = flat.shape[2]
    blocks = piece_rows // step
    per_level = n_layer * blocks
    n_tile = min(512, piece_rows)
    tokens = rows * CHUNKS
    share = tokens // n_tensor
    lanes = 2 * rank
    first_rows = rows // 2
    z = lax.axis_index("layer")
    t = lax.axis_index("tensor")
    d = lax.axis_index("dp")

    def nth_piece(i):
        return jnp.where(2 * z < n_layer, last - i, i)

    def raw_copy(n):
        level = layers - 1 - n // per_level
        i = (n // blocks) % n_layer
        start = pl.multiple_of(nth_piece(i) * piece_rows + (n % blocks) * step, step)
        return pltpu.make_async_copy(
            weight_hbm.at[level, pl.ds(start, step)], raw.at[n % RAW], raw_sem.at[n % RAW]
        )

    def relay(first, count):
        @pl.loop(first, first + count)
        def _(n):
            raw_copy(n).wait()

            @pl.when(n + RAW - 1 < layers * per_level)
            def _():
                raw_copy(n + RAW - 1).start()

            level = layers - 1 - n // per_level
            q = nth_piece((n // blocks) % n_layer)
            at = pl.ds(pl.multiple_of((n % blocks) * step, step), step)
            by_feature = jnp.swapaxes(raw[n % RAW], 0, 1)
            for a in range(n_tensor):
                flat[level % 2, q, at, a * width : (a + 1) * width] = by_feature[a]

    def span(c, count=1):
        return pl.ds(pl.multiple_of(c * rows, rows), count * rows)

    def feat_copy(level, c, shift):
        return pltpu.make_async_remote_copy(
            src_ref=feats.at[level % 2, t, span(c)],
            dst_ref=feats.at[level % 2, t, span(c)],
            send_sem=feat_send.at[level % 2, c, shift - 1],
            recv_sem=feat_recv.at[level % 2, c, shift - 1],
            device_id={"tensor": lax.rem(t + shift, n_tensor)},
            device_id_type=MESH,
        )

    def first_copy(half, shift):
        here = slice(half * first_rows, (half + 1) * first_rows)
        return pltpu.make_async_remote_copy(
            src_ref=feats.at[(layers - 1) % 2, t, here],
            dst_ref=feats.at[(layers - 1) % 2, t, here],
            send_sem=feat_send.at[(layers - 1) % 2, 0, shift - 1],
            recv_sem=first_recv.at[half, shift - 1],
            device_id={"tensor": lax.rem(t + shift, n_tensor)},
            device_id_type=MESH,
        )

    def right_copy(slot, level, c, q, first=0, count=rows):
        return pltpu.make_async_remote_copy(
            src_ref=part.at[slot, q, pl.ds(pl.multiple_of((c % 2) * rows + first, count), count)],
            dst_ref=from_left.at[level % 2, c, last - q, first : first + count],
            send_sem=part_send.at[slot, c % 2, q],
            recv_sem=left_recv.at[level % 2, c, last - q],
            device_id={"layer": z + 1},
            device_id_type=MESH,
        )

    def left_copy(slot, level, c, q, first=0, count=rows):
        return pltpu.make_async_remote_copy(
            src_ref=part.at[slot, q, pl.ds(pl.multiple_of((c % 2) * rows + first, count), count)],
            dst_ref=from_right.at[level % 2, c, q, first : first + count],
            send_sem=part_send.at[slot, c % 2, q],
            recv_sem=right_recv.at[level % 2, c, q],
            device_id={"layer": z - 1},
            device_id_type=MESH,
        )

    def wait_part_sends(slot, half):
        for q in range(n_layer):

            if q > 0:

                @pl.when(q > z)
                def _():
                    right_copy(slot, 0, half, q).wait_send()

            if q < last:

                @pl.when(q < z)
                def _():
                    left_copy(slot, 0, half, q).wait_send()

    def send_piece(slot, level, c, q, *part_rows):
        @pl.when((z == 0) & (q > 0))
        def _():
            right_copy(slot, level, c, q, *part_rows).start()

        @pl.when((z == last) & (q < last))
        def _():
            left_copy(slot, level, c, q, *part_rows).start()

    def multiply(slot, level, q, here, there):
        @pl.loop(0, piece_rows // n_tile)
        def _(j):
            at = pl.ds(pl.multiple_of(j * n_tile, n_tile), n_tile)
            acc = None
            for a in range(n_tensor):
                term = lax.dot_general(
                    feats[level % 2, a, here, :],
                    flat[level % 2, q, at, a * width : (a + 1) * width],
                    NT,
                    preferred_element_type=f32,
                )
                acc = term if acc is None else acc + term
            part[slot, q, there, at] = acc.astype(bf16)

    def forward(slot, level, c, s):
        right_piece, left_piece = last - s + z, s - last + z

        @pl.when((z > 0) & (right_piece <= last))
        def _():
            right_copy(slot, level, c, right_piece).wait_recv()

            @pl.when(right_piece > z)
            def _():
                part[slot, right_piece, span(c % 2), :] = (
                    part[slot, right_piece, span(c % 2), :].astype(f32)
                    + from_left[level % 2, c, last - right_piece].astype(f32)
                ).astype(bf16)
                right_copy(slot, level, c, right_piece).start()

        @pl.when((z < last) & (left_piece >= 0))
        def _():
            left_copy(slot, level, c, left_piece).wait_recv()

            @pl.when(left_piece < z)
            def _():
                part[slot, left_piece, span(c % 2), :] = (
                    part[slot, left_piece, span(c % 2), :].astype(f32)
                    + from_right[level % 2, c, left_piece].astype(f32)
                ).astype(bf16)
                left_copy(slot, level, c, left_piece).start()

    def grad_copy(c):
        return pltpu.make_async_copy(
            grad_hbm.at[pl.ds(c * rows, rows)], feats.at[(layers - 1) % 2, t, span(c)], io_sem.at[c]
        )

    def out_copy(c):
        return pltpu.make_async_copy(
            feats.at[1, t, span(c)], out_hbm.at[pl.ds(c * rows, rows)], io_sem.at[c]
        )

    def project(level, c):
        out_factor[level, c] = lax.dot_general(
            proj_out[level], feats[level % 2, t, span(c), :], NT, preferred_element_type=f32
        )

    def finish(slot, level, c):
        for shift in range(1, n_tensor):
            feat_copy(level, c, shift).wait_send()
        total[c] = total[c] + part[slot, z, span(c % 2), :].astype(f32)

        @pl.when(z > 0)
        def _():
            total[c] = total[c] + from_left[level % 2, c, last - z].astype(f32)

        @pl.when(z < last)
        def _():
            total[c] = total[c] + from_right[level % 2, c, z].astype(f32)

        feats[(level + 1) % 2, t, span(c), :] = total[c].astype(bf16)

        @pl.when(level > 0)
        def _():
            for shift in range(1, n_tensor):
                feat_copy(level - 1, c, shift).start()
            project(jnp.maximum(level - 1, 0), c)

        @pl.when(level == 0)
        def _():
            out_copy(c).start()

    def saved_copy(level):
        return pltpu.make_async_copy(saved_hbm.at[level], saved, load_sem.at[3])

    def share_of(i):
        return pl.ds(pl.multiple_of(i * share, share), share)

    def in_copy(shift):
        peer = lax.rem(t + shift, n_tensor)
        return pltpu.make_async_remote_copy(
            src_ref=in_mine.at[:, share_of(peer)],
            dst_ref=in_peer.at[shift - 1],
            send_sem=in_send_sem.at[shift - 1],
            recv_sem=in_recv_sem.at[shift - 1],
            device_id={"tensor": peer},
            device_id_type=MESH,
        )

    def run_copy(side):
        return pltpu.make_async_remote_copy(
            src_ref=run_send.at[side],
            dst_ref=run_recv.at[side],
            send_sem=run_send_sem.at[side],
            recv_sem=run_recv_sem.at[side],
            device_id={"layer": z + (1 if side == 0 else -1)},
            device_id_type=MESH,
        )

    def gather_copy(shift):
        return pltpu.make_async_remote_copy(
            src_ref=in_total.at[:, share_of(t)],
            dst_ref=in_total.at[:, share_of(t)],
            send_sem=gather_send_sem.at[shift - 1],
            recv_sem=gather_recv_sem.at[shift - 1],
            device_id={"tensor": lax.rem(t + shift, n_tensor)},
            device_id_type=MESH,
        )

    def owner_copy(shift):
        peer = lax.rem(z + shift, n_layer)
        return pltpu.make_async_remote_copy(
            src_ref=owner_send.at[peer],
            dst_ref=owner_recv.at[shift - 1],
            send_sem=owner_send_sem.at[shift - 1],
            recv_sem=owner_recv_sem.at[shift - 1],
            device_id={"layer": peer},
            device_id_type=MESH,
        )

    def tensor_copy(shift):
        return pltpu.make_async_remote_copy(
            src_ref=tensor_send,
            dst_ref=tensor_recv.at[shift - 1],
            send_sem=tensor_send_sem.at[shift - 1],
            recv_sem=tensor_recv_sem.at[shift - 1],
            device_id={"tensor": lax.rem(t + shift, n_tensor)},
            device_id_type=MESH,
        )

    def seq_copy(shift):
        return pltpu.make_async_remote_copy(
            src_ref=seq_blocks.at[0],
            dst_ref=seq_blocks.at[shift],
            send_sem=seq_send_sem.at[shift - 1],
            recv_sem=seq_recv_sem.at[shift - 1],
            device_id={"dp": lax.rem(d + shift, n_dp)},
            device_id_type=MESH,
        )

    def score_copy(shift):
        peer = lax.rem(z + shift, n_layer)
        return pltpu.make_async_remote_copy(
            src_ref=score_send.at[lax.rem(d - peer + n_dp, n_dp)],
            dst_ref=score_recv.at[shift - 1],
            send_sem=score_send_sem.at[shift - 1],
            recv_sem=score_recv_sem.at[shift - 1],
            device_id={"layer": peer},
            device_id_type=MESH,
        )

    def project_saved(level):
        saved_copy(level).wait()
        pair, half = level // 2, level % 2
        value = lax.dot_general(saved[...], proj_in[pair], NT, preferred_element_type=f32)
        if half == 0:
            in_mine[pair] = value.astype(bf16)
        else:
            lane = lax.broadcasted_iota(jnp.int32, value.shape, 1)
            in_mine[pair] = jnp.where(lane < rank, in_mine[pair].astype(f32), value).astype(bf16)
        if level + 1 < layers:
            saved_copy(level + 1).start()
        else:
            for shift in range(1, n_tensor):
                in_copy(shift).start()

    def run_step(s):
        if s == 0:
            value = in_mine[:, share_of(t)].astype(f32)
            for shift in range(1, n_tensor):
                in_copy(shift).wait()
                value = value + in_peer[shift - 1].astype(f32)
            in_sum[...] = value
        if s < last:

            @pl.when(z == s)
            def _():
                if s > 0:
                    run_copy(0).wait_recv()
                    run_send[0] = (in_sum[...] + run_recv[0].astype(f32)).astype(bf16)
                else:
                    run_send[0] = in_sum[...].astype(bf16)
                run_copy(0).start()

            @pl.when(z == last - s)
            def _():
                if s > 0:
                    run_copy(1).wait_recv()
                    run_send[1] = (in_sum[...] + run_recv[1].astype(f32)).astype(bf16)
                else:
                    run_send[1] = in_sum[...].astype(bf16)
                run_copy(1).start()

        else:

            @pl.when(z == last)
            def _():
                run_copy(0).wait_recv()

            @pl.when(z == 0)
            def _():
                run_copy(1).wait_recv()

            @pl.when(z < last)
            def _():
                run_copy(0).wait_send()
                in_sum[...] = in_sum[...] + run_recv[1].astype(f32)

            @pl.when(z > 0)
            def _():
                run_copy(1).wait_send()
                in_sum[...] = in_sum[...] + run_recv[0].astype(f32)

            in_total[:, share_of(t)] = in_sum[...].astype(bf16)
            for shift in range(1, n_tensor):
                gather_copy(shift).start()

    def send_blocks():
        for shift in range(1, n_tensor):
            gather_copy(shift).wait()
        lane = lax.broadcasted_iota(jnp.int32, (rank // 2, lanes), 1)
        for level in range(layers):
            pair, half = level // 2, level % 2
            acc = None
            for c in range(CHUNKS):
                term = lax.dot_general(
                    out_factor[level, c],
                    in_total[pair, c * rows : (c + 1) * rows].astype(f32),
                    NN,
                    precision=lax.Precision.HIGHEST,
                    preferred_element_type=f32,
                )
                acc = term if acc is None else acc + term
            block[...] = acc
            even = block[pl.ds(0, rank // 2, stride=2), :]
            odd = block[pl.ds(1, rank // 2, stride=2), :]
            if half == 0:
                odd = pltpu.roll(odd, rank, 1)
            else:
                even = pltpu.roll(even, rank, 1)
            level_blocks[level] = jnp.where(lane < rank, even, odd)
        for q in range(n_layer):
            level = jnp.int32(0)
            for k in range(1, layers):
                level = jnp.where(owner_ref[k] == q, k, level)
            owner_send[q] = level_blocks[level]
        for shift in range(1, n_layer):
            owner_copy(shift).start()

    def sum_layers():
        value = owner_send[z]
        for shift in range(1, n_layer):
            owner_copy(shift).wait()
            value = value + owner_recv[shift - 1]
        tensor_send[...] = value
        for shift in range(1, n_tensor):
            tensor_copy(shift).start()

    def sum_tensor():
        value = tensor_send[...]
        for shift in range(1, n_tensor):
            tensor_copy(shift).wait()
            value = value + tensor_recv[shift - 1]
        seq_blocks[0] = value
        for shift in range(1, n_dp):
            seq_copy(shift).start()

    def score():
        for shift in range(1, n_dp):
            seq_copy(shift).wait()
        pltpu.make_async_copy(query_hbm, queries, load_sem.at[2]).wait()
        acc = None
        for j in range(rank // 2):
            term = lax.dot_general(
                seq_blocks[:, j, :].astype(bf16),
                queries[:, j * lanes : (j + 1) * lanes],
                NT,
                preferred_element_type=f32,
            )
            acc = term if acc is None else acc + term
        for k in range(n_dp):
            score_send[k] = acc[k : k + 1]
        for shift in range(1, n_layer):
            score_copy(shift).start()

    def sum_scores():
        value = score_send[lax.rem(d - z + n_dp, n_dp)]
        for shift in range(1, n_layer):
            score_copy(shift).wait()
            value = value + score_recv[shift - 1]
        score_ref[...] = value

    barrier = pltpu.get_barrier_semaphore()

    @pl.when(z > 0)
    def _():
        pl.semaphore_signal(barrier, inc=1, device_id={"layer": z - 1}, device_id_type=MESH)

    @pl.when(z < last)
    def _():
        pl.semaphore_signal(barrier, inc=1, device_id={"layer": z + 1}, device_id_type=MESH)

    for axis, size, here in (("tensor", n_tensor, t), ("dp", n_dp, d)):
        for shift in range(1, size):
            pl.semaphore_signal(
                barrier, inc=1, device_id={axis: lax.rem(here + shift, size)}, device_id_type=MESH
            )

    for c in range(CHUNKS):
        grad_copy(c).start()
    for n in range(RAW - 1):
        raw_copy(n).start()
    pltpu.make_async_copy(proj_out_hbm, proj_out, load_sem.at[0]).start()
    pltpu.make_async_copy(proj_in_hbm, proj_in, load_sem.at[1]).start()
    pl.semaphore_wait(
        barrier, n_tensor + n_dp - 2 + jnp.minimum(z, 1) + jnp.minimum(last - z, 1)
    )

    for c in range(CHUNKS):
        grad_copy(c).wait()
        for shift in range(1, n_tensor):
            if c == 0:
                first_copy(0, shift).start()
                first_copy(1, shift).start()
            else:
                feat_copy(layers - 1, c, shift).start()

    phases = layers * CHUNKS
    fraction = per_level // (2 * CHUNKS)

    @pl.loop(0, phases - 1)
    def _(p):
        level = layers - 1 - p // CHUNKS
        c = p % CHUNKS
        slot = (p // 2) % 2
        old_level = layers - 1 - (p - 1) // CHUNKS
        old_c = (p + CHUNKS - 1) % CHUNKS
        old_slot = ((p - 1) // 2) % 2

        def at_phase(k, task, *args):
            @pl.when(p == k)
            def _():
                task(*args)

        @pl.when(p > 0)
        def _():
            forward(old_slot, old_level, old_c, 1)

        @pl.when(p == 0)
        def _():
            relay(0, blocks)
            q = nth_piece(0)
            for half in range(2):
                first = half * first_rows
                for shift in range(1, n_tensor):
                    first_copy(half, shift).wait_recv()
                multiply(slot, level, q, pl.ds(first, first_rows), pl.ds(first, first_rows))
                send_piece(slot, level, 0, q, first, first_rows)

            @pl.loop(1, n_layer)
            def _(i):
                relay(i * blocks, blocks)
                multiply(slot, level, nth_piece(i), pl.ds(0, rows), pl.ds(0, rows))
                send_piece(slot, level, 0, nth_piece(i))

        @pl.when(p == 1)
        def _():
            for shift in range(1, n_tensor):
                feat_copy(level, 1, shift).wait_recv()

            @pl.loop(0, n_layer)
            def _(i):
                multiply(slot, level, nth_piece(i), pl.ds(rows, rows), pl.ds(rows, rows))
                send_piece(slot, level, 1, nth_piece(i))

        @pl.when((p >= 2) & (c % 2 == 0))
        def _():
            @pl.when(p >= 4)
            def _():
                wait_part_sends(slot, 0)
                wait_part_sends(slot, 1)

            for shift in range(1, n_tensor):
                feat_copy(level, c, shift).wait_recv()
                feat_copy(level, c + 1, shift).wait_recv()

            @pl.loop(0, n_layer)
            def _(i):
                q = nth_piece(i)
                multiply(slot, level, q, span(c, 2), pl.ds(0, 2 * rows))
                send_piece(slot, level, c, q)

                @pl.when(p == phases - 2)
                def _():
                    send_piece(slot, level, c + 1, q)

            @pl.when(p < phases - 2)
            def _():
                for i in range(n_layer):
                    send_piece(slot, level, c + 1, nth_piece(i))

        base = (layers - level) * per_level + c * 2 * fraction
        early = jnp.where(p == 1, 2 * fraction, jnp.where(c % 2 == 1, fraction, 0))
        late = jnp.where((p == 1) | (c % 2 == 0), 2 * fraction, fraction)
        @pl.when(p == 0)
        def _():
            pltpu.make_async_copy(proj_out_hbm, proj_out, load_sem.at[0]).wait()
            pltpu.make_async_copy(proj_in_hbm, proj_in, load_sem.at[1]).wait()
            pltpu.make_async_copy(query_hbm, queries, load_sem.at[2]).start()
            saved_copy(0).start()
            for k in range(CHUNKS):
                total[k] = feats[(layers - 1) % 2, t, span(k), :].astype(f32)
                project(layers - 1, k)

        at_phase(phases - 3, send_blocks)

        @pl.when((p > 0) & (level > 0))
        def _():
            relay(jnp.where(p == 1, per_level, base), early)

        for s in range(2, n_layer - 1):

            @pl.when(p > 0)
            def _():
                forward(old_slot, old_level, old_c, s)

        for k in range(layers):
            at_phase(CHUNKS + k, project_saved, k)
        for k in range(n_layer):
            at_phase(CHUNKS + layers + k, run_step, k)
        at_phase(phases - 2, sum_layers)

        @pl.when((p > 0) & (level > 0))
        def _():
            relay(base + 2 * fraction - late, late)

        @pl.when(p > 0)
        def _():
            forward(old_slot, old_level, old_c, last)
            finish(old_slot, old_level, old_c)

    end_slot, end_level = ((phases - 1) // 2) % 2, jnp.int32(0)
    pair = (CHUNKS - 2, CHUNKS - 1)
    for s in range(1, last):
        for c in pair:
            forward(end_slot, end_level, c, s)
        if s == 1:
            sum_tensor()
    score()
    for c in pair:
        forward(end_slot, end_level, c, last)
        finish(end_slot, end_level, c)
    sum_scores()
    for k in range(2):
        wait_part_sends(k, 0)
        wait_part_sends(k, 1)
    for c in range(CHUNKS):
        out_copy(c).wait()


def on_device(saved_inputs, output_grad, weights, proj_in, proj_out, query_grads, owner_map):
    weights = weights[:, :, :, 0, :]
    layers, in_rows, n_tensor, width = weights.shape
    tokens = output_grad.shape[0]
    rank = proj_out.shape[1]
    n_queries = query_grads.shape[1]
    n_layer, n_dp = lax.axis_size("layer"), lax.axis_size("dp")
    assert tokens == LEN and n_dp == n_layer == layers and layers % 2 == 0
    rows = tokens // CHUNKS
    piece_rows = in_rows // n_layer
    step = min(256, piece_rows // 2)
    pairs, lanes, share = layers // 2, 2 * rank, tokens // n_tensor
    bf16, f32 = jnp.bfloat16, jnp.float32
    dma = pltpu.SemaphoreType.DMA
    hops = n_layer - 1
    anywhere = pl.BlockSpec(memory_space=pl.ANY)
    return pl.pallas_call(
        functools.partial(
            stack_kernel, (layers, n_layer, n_tensor, n_dp, rows, width, rank, step)
        ),
        out_shape=(
            jax.ShapeDtypeStruct((tokens, width), bf16),
            jax.ShapeDtypeStruct((1, n_queries), f32),
        ),
        in_specs=[pl.BlockSpec(memory_space=pltpu.SMEM)] + [anywhere] * 6,
        out_specs=(anywhere, pl.BlockSpec(memory_space=pltpu.VMEM)),
        scratch_shapes=[
            pltpu.VMEM((RAW, step, n_tensor, width), bf16),
            pltpu.VMEM((2, n_layer, piece_rows, n_tensor * width), bf16),
            pltpu.VMEM((2, n_tensor, tokens, width), bf16),
            pltpu.VMEM((2, n_layer, 2 * rows, piece_rows), bf16),
            pltpu.VMEM((2, CHUNKS, hops, rows, piece_rows), bf16),
            pltpu.VMEM((2, CHUNKS, hops, rows, piece_rows), bf16),
            pltpu.VMEM((CHUNKS, rows, width), f32),
            pltpu.VMEM((pairs, lanes, width), bf16),
            pltpu.VMEM((layers, rank, width), bf16),
            pltpu.VMEM(query_grads.shape[1:], bf16),
            pltpu.VMEM((tokens, width), bf16),
            pltpu.VMEM((layers, CHUNKS, rank, rows), f32),
            pltpu.VMEM((pairs, tokens, lanes), bf16),
            pltpu.VMEM((n_tensor - 1, pairs, share, lanes), bf16),
            pltpu.VMEM((pairs, share, lanes), f32),
            pltpu.VMEM((2, pairs, share, lanes), bf16),
            pltpu.VMEM((2, pairs, share, lanes), bf16),
            pltpu.VMEM((pairs, tokens, lanes), bf16),
            pltpu.VMEM((rank, lanes), f32),
            pltpu.VMEM((layers, rank // 2, lanes), f32),
            pltpu.VMEM((n_layer, rank // 2, lanes), f32),
            pltpu.VMEM((hops, rank // 2, lanes), f32),
            pltpu.VMEM((rank // 2, lanes), f32),
            pltpu.VMEM((n_tensor - 1, rank // 2, lanes), f32),
            pltpu.VMEM((n_dp, rank // 2, lanes), f32),
            pltpu.VMEM((n_dp, 1, n_queries), f32),
            pltpu.VMEM((hops, 1, n_queries), f32),
            dma((RAW,)),
            dma((CHUNKS,)),
            dma((4,)),
            dma((2, CHUNKS, n_tensor - 1)),
            dma((2, CHUNKS, n_tensor - 1)),
            dma((2, n_tensor - 1)),
            dma((2, 2, n_layer)),
            dma((2, CHUNKS, hops)),
            dma((2, CHUNKS, hops)),
            dma((n_tensor - 1,)),
            dma((n_tensor - 1,)),
            dma((2,)),
            dma((2,)),
            dma((n_tensor - 1,)),
            dma((n_tensor - 1,)),
            dma((hops,)),
            dma((hops,)),
            dma((n_tensor - 1,)),
            dma((n_tensor - 1,)),
            dma((n_dp - 1,)),
            dma((n_dp - 1,)),
            dma((hops,)),
            dma((hops,)),
        ],
        compiler_params=pltpu.CompilerParams(
            collective_id=0, has_side_effects=True, vmem_limit_bytes=VMEM_BYTES
        ),
        name="backward_stack",
    )(
        owner_map,
        output_grad,
        weights,
        saved_inputs,
        proj_in.reshape(pairs, lanes, width),
        proj_out,
        query_grads[0],
    )


def solution(mesh):
    in_specs = (
        P(None, "dp", ("tensor", "layer")),
        P("dp", ("tensor", "layer")),
        P(None, "tensor", None, "layer", None),
        P(None, None, ("tensor", "layer")),
        P(None, None, ("tensor", "layer")),
        P("layer", ("dp", "tensor"), None),
        P(),
    )
    out_specs = (P("dp", ("tensor", "layer")), P("layer", ("dp", "tensor")))
    return jax.shard_map(
        on_device, mesh=mesh, in_specs=in_specs, out_specs=out_specs, check_vma=False
    )
```

```python
import functools

import jax
import jax.numpy as jnp
from jax import lax
from jax.experimental import pallas as pl
from jax.experimental.pallas import tpu as pltpu
from jax.sharding import PartitionSpec as P

LEN = 512
CHUNKS = 4
RAW = 3
FIRST = 4
MESH = pl.DeviceIdType.MESH
VMEM_BYTES = 67_000_000
NT = (((1,), (1,)), ((), ()))
NN = (((1,), (0,)), ((), ()))


def stack_kernel(
    dims,
    owner_ref,
    grad_hbm,
    weight_hbm,
    saved_hbm,
    proj_in_hbm,
    proj_out_hbm,
    query_hbm,
    out_hbm,
    score_hbm,
    raw,
    flat,
    ahead,
    feats,
    part,
    from_left,
    from_right,
    total,
    proj_in,
    proj_out,
    queries,
    saved,
    out_factor,
    in_mine,
    in_peer,
    in_sum,
    run_send,
    run_recv,
    in_total,
    block,
    level_blocks,
    owner_send,
    owner_recv,
    tensor_send,
    tensor_recv,
    seq_blocks,
    score_send,
    score_recv,
    score_total,
    raw_sem,
    io_sem,
    load_sem,
    feat_send,
    feat_recv,
    first_recv,
    part_send,
    left_recv,
    right_recv,
    in_send_sem,
    in_recv_sem,
    run_send_sem,
    run_recv_sem,
    gather_send_sem,
    gather_recv_sem,
    owner_send_sem,
    owner_recv_sem,
    tensor_send_sem,
    tensor_recv_sem,
    seq_send_sem,
    seq_recv_sem,
    score_send_sem,
    score_recv_sem,
):
    layers, n_layer, n_tensor, n_dp, rows, width, rank, step = dims
    last = n_layer - 1
    f32, bf16 = jnp.float32, jnp.bfloat16
    piece_rows = flat.shape[2]
    blocks = piece_rows // step
    per_level = n_layer * blocks
    n_tile = min(512, piece_rows)
    tokens = rows * CHUNKS
    share = tokens // n_tensor
    lanes = 2 * rank
    first_rows = rows // FIRST
    z = lax.axis_index("layer")
    t = lax.axis_index("tensor")
    d = lax.axis_index("dp")

    def nth_piece(i):
        return jnp.where(2 * z < n_layer, last - i, i)

    def raw_copy(n):
        level = layers - 1 - n // per_level
        i = (n // blocks) % n_layer
        start = pl.multiple_of(nth_piece(i) * piece_rows + (n % blocks) * step, step)
        return pltpu.make_async_copy(
            weight_hbm.at[level, pl.ds(start, step)], raw.at[n % RAW], raw_sem.at[n % RAW]
        )

    def relay(first, count):
        @pl.loop(first, first + count)
        def _(n):
            raw_copy(n).wait()

            @pl.when(n + RAW - 1 < layers * per_level)
            def _():
                raw_copy(n + RAW - 1).start()

            level = layers - 1 - n // per_level
            q = nth_piece((n // blocks) % n_layer)
            at = pl.ds(pl.multiple_of((n % blocks) * step, step), step)
            by_feature = jnp.swapaxes(raw[n % RAW], 0, 1)
            for a in range(n_tensor):
                flat[level % 2, q, at, a * width : (a + 1) * width] = by_feature[a]

    def span(c, count=1):
        return pl.ds(pl.multiple_of(c * rows, rows), count * rows)

    def feat_copy(level, c, shift):
        return pltpu.make_async_remote_copy(
            src_ref=feats.at[level % 2, t, span(c)],
            dst_ref=feats.at[level % 2, t, span(c)],
            send_sem=feat_send.at[level % 2, c, shift - 1],
            recv_sem=feat_recv.at[level % 2, c, shift - 1],
            device_id={"tensor": lax.rem(t + shift, n_tensor)},
            device_id_type=MESH,
        )

    def first_copy(half, shift):
        here = slice(half * first_rows, (half + 1) * first_rows)
        return pltpu.make_async_remote_copy(
            src_ref=feats.at[(layers - 1) % 2, t, here],
            dst_ref=feats.at[(layers - 1) % 2, t, here],
            send_sem=feat_send.at[(layers - 1) % 2, 0, shift - 1],
            recv_sem=first_recv.at[half, shift - 1],
            device_id={"tensor": lax.rem(t + shift, n_tensor)},
            device_id_type=MESH,
        )

    def right_copy(slot, level, c, q, first=0, count=rows):
        return pltpu.make_async_remote_copy(
            src_ref=part.at[slot, q, pl.ds(pl.multiple_of((c % 2) * rows + first, count), count)],
            dst_ref=from_left.at[level % 2, c, last - q, first : first + count],
            send_sem=part_send.at[slot, c % 2, q],
            recv_sem=left_recv.at[level % 2, c, last - q],
            device_id={"layer": z + 1},
            device_id_type=MESH,
        )

    def left_copy(slot, level, c, q, first=0, count=rows):
        return pltpu.make_async_remote_copy(
            src_ref=part.at[slot, q, pl.ds(pl.multiple_of((c % 2) * rows + first, count), count)],
            dst_ref=from_right.at[level % 2, c, q, first : first + count],
            send_sem=part_send.at[slot, c % 2, q],
            recv_sem=right_recv.at[level % 2, c, q],
            device_id={"layer": z - 1},
            device_id_type=MESH,
        )

    def wait_part_sends(slot, half):
        for q in range(n_layer):

            if q > 0:

                @pl.when(q > z)
                def _():
                    right_copy(slot, 0, half, q).wait_send()

            if q < last:

                @pl.when(q < z)
                def _():
                    left_copy(slot, 0, half, q).wait_send()

    def send_piece(slot, level, c, q, *part_rows):
        @pl.when((z == 0) & (q > 0))
        def _():
            right_copy(slot, level, c, q, *part_rows).start()

        @pl.when((z == last) & (q < last))
        def _():
            left_copy(slot, level, c, q, *part_rows).start()

    def multiply(slot, level, q, here, there):
        @pl.loop(0, piece_rows // n_tile)
        def _(j):
            at = pl.ds(pl.multiple_of(j * n_tile, n_tile), n_tile)
            acc = None
            for a in range(n_tensor):
                term = lax.dot_general(
                    feats[level % 2, a, here, :],
                    flat[level % 2, q, at, a * width : (a + 1) * width],
                    NT,
                    preferred_element_type=f32,
                )
                acc = term if acc is None else acc + term
            part[slot, q, there, at] = acc.astype(bf16)

    def start_piece(slot, level, q):
        def features_of(a):
            return pl.ds(pl.multiple_of(a * width, width), width)

        @pl.loop(0, piece_rows // n_tile)
        def _(j):
            at = pl.ds(pl.multiple_of(j * n_tile, n_tile), n_tile)
            ahead[:, at] = lax.dot_general(
                feats[level % 2, t, 0:rows, :],
                flat[level % 2, q, at, features_of(t)],
                NT,
                preferred_element_type=f32,
            )

        for k in range(FIRST):
            here = slice(k * first_rows, (k + 1) * first_rows)
            for shift in range(1, n_tensor):
                first_copy(k, shift).wait_recv()

            @pl.loop(0, piece_rows // n_tile)
            def _(j):
                at = pl.ds(pl.multiple_of(j * n_tile, n_tile), n_tile)
                acc = ahead[here, at]
                for shift in range(1, n_tensor):
                    a = lax.rem(t + shift, n_tensor)
                    acc = acc + lax.dot_general(
                        feats[level % 2, a, here, :],
                        flat[level % 2, q, at, features_of(a)],
                        NT,
                        preferred_element_type=f32,
                    )
                part[slot, q, here, at] = acc.astype(bf16)

            send_piece(slot, level, 0, q, k * first_rows, first_rows)

    def forward(slot, level, c, s):
        right_piece, left_piece = last - s + z, s - last + z

        @pl.when((z > 0) & (right_piece <= last))
        def _():
            right_copy(slot, level, c, right_piece).wait_recv()

            @pl.when(right_piece > z)
            def _():
                part[slot, right_piece, span(c % 2), :] = (
                    part[slot, right_piece, span(c % 2), :].astype(f32)
                    + from_left[level % 2, c, last - right_piece].astype(f32)
                ).astype(bf16)
                right_copy(slot, level, c, right_piece).start()

        @pl.when((z < last) & (left_piece >= 0))
        def _():
            left_copy(slot, level, c, left_piece).wait_recv()

            @pl.when(left_piece < z)
            def _():
                part[slot, left_piece, span(c % 2), :] = (
                    part[slot, left_piece, span(c % 2), :].astype(f32)
                    + from_right[level % 2, c, left_piece].astype(f32)
                ).astype(bf16)
                left_copy(slot, level, c, left_piece).start()

    def grad_copy(c):
        return pltpu.make_async_copy(
            grad_hbm.at[pl.ds(c * rows, rows)], feats.at[(layers - 1) % 2, t, span(c)], io_sem.at[c]
        )

    def out_copy(c):
        return pltpu.make_async_copy(
            feats.at[1, t, span(c)], out_hbm.at[pl.ds(c * rows, rows)], io_sem.at[c]
        )

    def project(level, c):
        out_factor[level, c] = lax.dot_general(
            proj_out[level], feats[level % 2, t, span(c), :], NT, preferred_element_type=f32
        )

    def finish(slot, level, c):
        for shift in range(1, n_tensor):
            feat_copy(level, c, shift).wait_send()
        total[c] = total[c] + part[slot, z, span(c % 2), :].astype(f32)

        @pl.when(z > 0)
        def _():
            total[c] = total[c] + from_left[level % 2, c, last - z].astype(f32)

        @pl.when(z < last)
        def _():
            total[c] = total[c] + from_right[level % 2, c, z].astype(f32)

        feats[(level + 1) % 2, t, span(c), :] = total[c].astype(bf16)

        @pl.when(level > 0)
        def _():
            for shift in range(1, n_tensor):
                feat_copy(level - 1, c, shift).start()
            project(jnp.maximum(level - 1, 0), c)

        @pl.when(level == 0)
        def _():
            out_copy(c).start()

    def saved_copy(level):
        return pltpu.make_async_copy(saved_hbm.at[level], saved, load_sem.at[3])

    def share_of(i):
        return pl.ds(pl.multiple_of(i * share, share), share)

    def in_copy(shift):
        peer = lax.rem(t + shift, n_tensor)
        return pltpu.make_async_remote_copy(
            src_ref=in_mine.at[:, share_of(peer)],
            dst_ref=in_peer.at[shift - 1],
            send_sem=in_send_sem.at[shift - 1],
            recv_sem=in_recv_sem.at[shift - 1],
            device_id={"tensor": peer},
            device_id_type=MESH,
        )

    def run_copy(side):
        return pltpu.make_async_remote_copy(
            src_ref=run_send.at[side],
            dst_ref=run_recv.at[side],
            send_sem=run_send_sem.at[side],
            recv_sem=run_recv_sem.at[side],
            device_id={"layer": z + (1 if side == 0 else -1)},
            device_id_type=MESH,
        )

    def gather_copy(shift):
        return pltpu.make_async_remote_copy(
            src_ref=in_total.at[:, share_of(t)],
            dst_ref=in_total.at[:, share_of(t)],
            send_sem=gather_send_sem.at[shift - 1],
            recv_sem=gather_recv_sem.at[shift - 1],
            device_id={"tensor": lax.rem(t + shift, n_tensor)},
            device_id_type=MESH,
        )

    def owner_copy(shift):
        peer = lax.rem(z + shift, n_layer)
        return pltpu.make_async_remote_copy(
            src_ref=owner_send.at[peer],
            dst_ref=owner_recv.at[shift - 1],
            send_sem=owner_send_sem.at[shift - 1],
            recv_sem=owner_recv_sem.at[shift - 1],
            device_id={"layer": peer},
            device_id_type=MESH,
        )

    def tensor_copy(shift):
        return pltpu.make_async_remote_copy(
            src_ref=tensor_send,
            dst_ref=tensor_recv.at[shift - 1],
            send_sem=tensor_send_sem.at[shift - 1],
            recv_sem=tensor_recv_sem.at[shift - 1],
            device_id={"tensor": lax.rem(t + shift, n_tensor)},
            device_id_type=MESH,
        )

    def seq_copy(shift):
        return pltpu.make_async_remote_copy(
            src_ref=seq_blocks.at[0],
            dst_ref=seq_blocks.at[shift],
            send_sem=seq_send_sem.at[shift - 1],
            recv_sem=seq_recv_sem.at[shift - 1],
            device_id={"dp": lax.rem(d + shift, n_dp)},
            device_id_type=MESH,
        )

    def score_copy(shift):
        peer = lax.rem(z + shift, n_layer)
        return pltpu.make_async_remote_copy(
            src_ref=score_send.at[lax.rem(d - peer + n_dp, n_dp)],
            dst_ref=score_recv.at[shift - 1],
            send_sem=score_send_sem.at[shift - 1],
            recv_sem=score_recv_sem.at[shift - 1],
            device_id={"layer": peer},
            device_id_type=MESH,
        )

    def project_saved(level):
        saved_copy(level).wait()
        pair, half = level // 2, level % 2
        value = lax.dot_general(saved[...], proj_in[pair], NT, preferred_element_type=f32)
        if half == 0:
            in_mine[pair] = value.astype(bf16)
        else:
            lane = lax.broadcasted_iota(jnp.int32, value.shape, 1)
            in_mine[pair] = jnp.where(lane < rank, in_mine[pair].astype(f32), value).astype(bf16)
        if level + 1 < layers:
            saved_copy(level + 1).start()
        else:
            for shift in range(1, n_tensor):
                in_copy(shift).start()

    def run_step(s):
        if s == 0:
            value = in_mine[:, share_of(t)].astype(f32)
            for shift in range(1, n_tensor):
                in_copy(shift).wait()
                value = value + in_peer[shift - 1].astype(f32)
            in_sum[...] = value
        if s < last:

            @pl.when(z == s)
            def _():
                if s > 0:
                    run_copy(0).wait_recv()
                    run_send[0] = (in_sum[...] + run_recv[0].astype(f32)).astype(bf16)
                else:
                    run_send[0] = in_sum[...].astype(bf16)
                run_copy(0).start()

            @pl.when(z == last - s)
            def _():
                if s > 0:
                    run_copy(1).wait_recv()
                    run_send[1] = (in_sum[...] + run_recv[1].astype(f32)).astype(bf16)
                else:
                    run_send[1] = in_sum[...].astype(bf16)
                run_copy(1).start()

        else:

            @pl.when(z == last)
            def _():
                run_copy(0).wait_recv()

            @pl.when(z == 0)
            def _():
                run_copy(1).wait_recv()

            @pl.when(z < last)
            def _():
                run_copy(0).wait_send()
                in_sum[...] = in_sum[...] + run_recv[1].astype(f32)

            @pl.when(z > 0)
            def _():
                run_copy(1).wait_send()
                in_sum[...] = in_sum[...] + run_recv[0].astype(f32)

            in_total[:, share_of(t)] = in_sum[...].astype(bf16)
            for shift in range(1, n_tensor):
                gather_copy(shift).start()

    def send_blocks():
        for shift in range(1, n_tensor):
            gather_copy(shift).wait()
        lane = lax.broadcasted_iota(jnp.int32, (rank // 2, lanes), 1)
        for level in range(layers):
            pair, half = level // 2, level % 2
            acc = None
            for c in range(CHUNKS):
                term = lax.dot_general(
                    out_factor[level, c],
                    in_total[pair, c * rows : (c + 1) * rows].astype(f32),
                    NN,
                    precision=lax.Precision.HIGHEST,
                    preferred_element_type=f32,
                )
                acc = term if acc is None else acc + term
            block[...] = acc
            even = block[pl.ds(0, rank // 2, stride=2), :]
            odd = block[pl.ds(1, rank // 2, stride=2), :]
            if half == 0:
                odd = pltpu.roll(odd, rank, 1)
            else:
                even = pltpu.roll(even, rank, 1)
            level_blocks[level] = jnp.where(lane < rank, even, odd)
        for q in range(n_layer):
            level = jnp.int32(0)
            for k in range(1, layers):
                level = jnp.where(owner_ref[k] == q, k, level)
            owner_send[q] = level_blocks[level]
        for shift in range(1, n_layer):
            owner_copy(shift).start()

    def sum_layers():
        value = owner_send[z]
        for shift in range(1, n_layer):
            owner_copy(shift).wait()
            value = value + owner_recv[shift - 1]
        tensor_send[...] = value
        for shift in range(1, n_tensor):
            tensor_copy(shift).start()

    def sum_tensor():
        value = tensor_send[...]
        for shift in range(1, n_tensor):
            tensor_copy(shift).wait()
            value = value + tensor_recv[shift - 1]
        seq_blocks[0] = value
        for shift in range(1, n_dp):
            seq_copy(shift).start()

    def score():
        for shift in range(1, n_dp):
            seq_copy(shift).wait()
        pltpu.make_async_copy(query_hbm, queries, load_sem.at[2]).wait()
        acc = None
        for j in range(rank // 2):
            term = lax.dot_general(
                seq_blocks[:, j, :].astype(bf16),
                queries[:, j * lanes : (j + 1) * lanes],
                NT,
                preferred_element_type=f32,
            )
            acc = term if acc is None else acc + term
        for k in range(n_dp):
            score_send[k] = acc[k : k + 1]
        for shift in range(1, n_layer):
            score_copy(shift).start()

    def score_out():
        return pltpu.make_async_copy(score_total, score_hbm, load_sem.at[4])

    def sum_scores():
        value = score_send[lax.rem(d - z + n_dp, n_dp)]
        for shift in range(1, n_layer):
            score_copy(shift).wait()
            value = value + score_recv[shift - 1]
        score_total[...] = value
        score_out().start()

    barrier = pltpu.get_barrier_semaphore()

    @pl.when(z > 0)
    def _():
        pl.semaphore_signal(barrier, inc=1, device_id={"layer": z - 1}, device_id_type=MESH)

    @pl.when(z < last)
    def _():
        pl.semaphore_signal(barrier, inc=1, device_id={"layer": z + 1}, device_id_type=MESH)

    for axis, size, here in (("tensor", n_tensor, t), ("dp", n_dp, d)):
        for shift in range(1, size):
            pl.semaphore_signal(
                barrier, inc=1, device_id={axis: lax.rem(here + shift, size)}, device_id_type=MESH
            )

    for c in range(CHUNKS):
        grad_copy(c).start()
    for n in range(RAW - 1):
        raw_copy(n).start()
    pltpu.make_async_copy(proj_out_hbm, proj_out, load_sem.at[0]).start()
    pltpu.make_async_copy(proj_in_hbm, proj_in, load_sem.at[1]).start()
    pl.semaphore_wait(
        barrier, n_tensor + n_dp - 2 + jnp.minimum(z, 1) + jnp.minimum(last - z, 1)
    )

    for c in range(CHUNKS):
        grad_copy(c).wait()
        for shift in range(1, n_tensor):
            if c == 0:
                for k in range(FIRST):
                    first_copy(k, shift).start()
            else:
                feat_copy(layers - 1, c, shift).start()

    phases = layers * CHUNKS
    fraction = per_level // (2 * CHUNKS)

    @pl.loop(0, phases - 1)
    def _(p):
        level = layers - 1 - p // CHUNKS
        c = p % CHUNKS
        slot = (p // 2) % 2
        old_level = layers - 1 - (p - 1) // CHUNKS
        old_c = (p + CHUNKS - 1) % CHUNKS
        old_slot = ((p - 1) // 2) % 2

        def at_phase(k, task, *args):
            @pl.when(p == k)
            def _():
                task(*args)

        @pl.when(p > 0)
        def _():
            forward(old_slot, old_level, old_c, 1)

        @pl.when(p == 0)
        def _():
            relay(0, blocks)
            start_piece(slot, level, nth_piece(0))

            @pl.loop(1, n_layer)
            def _(i):
                relay(i * blocks, blocks)
                multiply(slot, level, nth_piece(i), pl.ds(0, rows), pl.ds(0, rows))
                send_piece(slot, level, 0, nth_piece(i))

        @pl.when(p == 1)
        def _():
            for shift in range(1, n_tensor):
                feat_copy(level, 1, shift).wait_recv()

            @pl.loop(0, n_layer)
            def _(i):
                multiply(slot, level, nth_piece(i), pl.ds(rows, rows), pl.ds(rows, rows))
                send_piece(slot, level, 1, nth_piece(i))

        @pl.when((p >= 2) & (c % 2 == 0))
        def _():
            @pl.when(p >= 4)
            def _():
                wait_part_sends(slot, 0)
                wait_part_sends(slot, 1)

            for shift in range(1, n_tensor):
                feat_copy(level, c, shift).wait_recv()
                feat_copy(level, c + 1, shift).wait_recv()

            @pl.loop(0, n_layer)
            def _(i):
                q = nth_piece(i)
                multiply(slot, level, q, span(c, 2), pl.ds(0, 2 * rows))
                send_piece(slot, level, c, q)

                @pl.when(p == phases - 2)
                def _():
                    send_piece(slot, level, c + 1, q)

            @pl.when(p < phases - 2)
            def _():
                for i in range(n_layer):
                    send_piece(slot, level, c + 1, nth_piece(i))

        base = (layers - level) * per_level + c * 2 * fraction
        early = jnp.where(p == 1, 2 * fraction, jnp.where(c % 2 == 1, fraction, 0))
        late = jnp.where((p == 1) | (c % 2 == 0), 2 * fraction, fraction)
        @pl.when(p == 0)
        def _():
            pltpu.make_async_copy(proj_out_hbm, proj_out, load_sem.at[0]).wait()
            pltpu.make_async_copy(proj_in_hbm, proj_in, load_sem.at[1]).wait()
            pltpu.make_async_copy(query_hbm, queries, load_sem.at[2]).start()
            saved_copy(0).start()
            for k in range(CHUNKS):
                total[k] = feats[(layers - 1) % 2, t, span(k), :].astype(f32)
                project(layers - 1, k)

        at_phase(phases - 3, send_blocks)

        @pl.when((p > 0) & (level > 0))
        def _():
            relay(jnp.where(p == 1, per_level, base), early)

        for s in range(2, n_layer - 1):

            @pl.when(p > 0)
            def _():
                forward(old_slot, old_level, old_c, s)

        for k in range(layers):
            at_phase(CHUNKS + k, project_saved, k)
        for k in range(n_layer):
            at_phase(CHUNKS + layers + k, run_step, k)
        at_phase(phases - 2, sum_layers)

        @pl.when((p > 0) & (level > 0))
        def _():
            relay(base + 2 * fraction - late, late)

        @pl.when(p > 0)
        def _():
            forward(old_slot, old_level, old_c, last)
            finish(old_slot, old_level, old_c)

    end_slot, end_level = ((phases - 1) // 2) % 2, jnp.int32(0)
    pair = (CHUNKS - 2, CHUNKS - 1)
    for s in range(1, last):
        for c in pair:
            forward(end_slot, end_level, c, s)
        if s == 1:
            sum_tensor()
    score()
    for c in pair:
        forward(end_slot, end_level, c, last)
        finish(end_slot, end_level, c)
    sum_scores()
    for k in range(2):
        wait_part_sends(k, 0)
        wait_part_sends(k, 1)
    score_out().wait()
    for c in range(CHUNKS):
        out_copy(c).wait()


def hand_over_kernel(grad_in, score_in, grad_out, score_out, grad, score, in_sem, out_sem):
    count = in_sem.shape[0] - 1
    rows = grad.shape[0] // count

    def copies(source, target, sem):
        for k in range(count):
            at = pl.ds(k * rows, rows)
            yield pltpu.make_async_copy(source[0].at[at], target[0].at[at], sem.at[k])
        yield pltpu.make_async_copy(source[1], target[1], sem.at[count])

    loads = list(copies((grad_in, score_in), (grad, score), in_sem))
    stores = list(copies((grad, score), (grad_out, score_out), out_sem))
    for load in loads:
        load.start()
    for load, store in zip(loads, stores):
        load.wait()
        store.start()
    for store in stores:
        store.wait()


def hand_over(grad, score):
    shapes = tuple(jax.ShapeDtypeStruct(x.shape, x.dtype) for x in (grad, score))
    anywhere = pl.BlockSpec(memory_space=pl.ANY)
    return pl.pallas_call(
        hand_over_kernel,
        out_shape=shapes,
        in_specs=[anywhere] * 2,
        out_specs=(anywhere,) * 2,
        scratch_shapes=[
            pltpu.VMEM(grad.shape, grad.dtype),
            pltpu.VMEM(score.shape, score.dtype),
            pltpu.SemaphoreType.DMA((CHUNKS + 1,)),
            pltpu.SemaphoreType.DMA((CHUNKS + 1,)),
        ],
        name="hand_over",
    )(grad, score)


def on_device(saved_inputs, output_grad, weights, proj_in, proj_out, query_grads, owner_map):
    weights = weights[:, :, :, 0, :]
    layers, in_rows, n_tensor, width = weights.shape
    tokens = output_grad.shape[0]
    rank = proj_out.shape[1]
    n_queries = query_grads.shape[1]
    n_layer, n_dp = lax.axis_size("layer"), lax.axis_size("dp")
    assert tokens == LEN and n_dp == n_layer == layers and layers % 2 == 0
    rows = tokens // CHUNKS
    piece_rows = in_rows // n_layer
    step = min(256, piece_rows // 2)
    pairs, lanes, share = layers // 2, 2 * rank, tokens // n_tensor
    bf16, f32 = jnp.bfloat16, jnp.float32
    dma = pltpu.SemaphoreType.DMA
    hops = n_layer - 1
    anywhere = pl.BlockSpec(memory_space=pl.ANY)
    results = pl.pallas_call(
        functools.partial(
            stack_kernel, (layers, n_layer, n_tensor, n_dp, rows, width, rank, step)
        ),
        out_shape=(
            jax.ShapeDtypeStruct((tokens, width), bf16),
            jax.ShapeDtypeStruct((1, n_queries), f32),
        ),
        in_specs=[pl.BlockSpec(memory_space=pltpu.SMEM)] + [anywhere] * 6,
        out_specs=(anywhere, anywhere),
        scratch_shapes=[
            pltpu.VMEM((RAW, step, n_tensor, width), bf16),
            pltpu.VMEM((2, n_layer, piece_rows, n_tensor * width), bf16),
            pltpu.VMEM((rows, piece_rows), f32),
            pltpu.VMEM((2, n_tensor, tokens, width), bf16),
            pltpu.VMEM((2, n_layer, 2 * rows, piece_rows), bf16),
            pltpu.VMEM((2, CHUNKS, hops, rows, piece_rows), bf16),
            pltpu.VMEM((2, CHUNKS, hops, rows, piece_rows), bf16),
            pltpu.VMEM((CHUNKS, rows, width), f32),
            pltpu.VMEM((pairs, lanes, width), bf16),
            pltpu.VMEM((layers, rank, width), bf16),
            pltpu.VMEM(query_grads.shape[1:], bf16),
            pltpu.VMEM((tokens, width), bf16),
            pltpu.VMEM((layers, CHUNKS, rank, rows), f32),
            pltpu.VMEM((pairs, tokens, lanes), bf16),
            pltpu.VMEM((n_tensor - 1, pairs, share, lanes), bf16),
            pltpu.VMEM((pairs, share, lanes), f32),
            pltpu.VMEM((2, pairs, share, lanes), bf16),
            pltpu.VMEM((2, pairs, share, lanes), bf16),
            pltpu.VMEM((pairs, tokens, lanes), bf16),
            pltpu.VMEM((rank, lanes), f32),
            pltpu.VMEM((layers, rank // 2, lanes), f32),
            pltpu.VMEM((n_layer, rank // 2, lanes), f32),
            pltpu.VMEM((hops, rank // 2, lanes), f32),
            pltpu.VMEM((rank // 2, lanes), f32),
            pltpu.VMEM((n_tensor - 1, rank // 2, lanes), f32),
            pltpu.VMEM((n_dp, rank // 2, lanes), f32),
            pltpu.VMEM((n_dp, 1, n_queries), f32),
            pltpu.VMEM((hops, 1, n_queries), f32),
            pltpu.VMEM((1, n_queries), f32),
            dma((RAW,)),
            dma((CHUNKS,)),
            dma((5,)),
            dma((2, CHUNKS, n_tensor - 1)),
            dma((2, CHUNKS, n_tensor - 1)),
            dma((FIRST, n_tensor - 1)),
            dma((2, 2, n_layer)),
            dma((2, CHUNKS, hops)),
            dma((2, CHUNKS, hops)),
            dma((n_tensor - 1,)),
            dma((n_tensor - 1,)),
            dma((2,)),
            dma((2,)),
            dma((n_tensor - 1,)),
            dma((n_tensor - 1,)),
            dma((hops,)),
            dma((hops,)),
            dma((n_tensor - 1,)),
            dma((n_tensor - 1,)),
            dma((n_dp - 1,)),
            dma((n_dp - 1,)),
            dma((hops,)),
            dma((hops,)),
        ],
        compiler_params=pltpu.CompilerParams(
            collective_id=0, has_side_effects=True, vmem_limit_bytes=VMEM_BYTES
        ),
        name="backward_stack",
    )(
        owner_map,
        output_grad,
        weights,
        saved_inputs,
        proj_in.reshape(pairs, lanes, width),
        proj_out,
        query_grads[0],
    )
    return hand_over(*results)


def solution(mesh):
    in_specs = (
        P(None, "dp", ("tensor", "layer")),
        P("dp", ("tensor", "layer")),
        P(None, "tensor", None, "layer", None),
        P(None, None, ("tensor", "layer")),
        P(None, None, ("tensor", "layer")),
        P("layer", ("dp", "tensor"), None),
        P(),
    )
    out_specs = (P("dp", ("tensor", "layer")), P("layer", ("dp", "tensor")))
    return jax.shard_map(
        on_device, mesh=mesh, in_specs=in_specs, out_specs=out_specs, check_vma=False
    )
```

```python
import functools

import jax
import jax.numpy as jnp
from jax import lax
from jax.experimental import pallas as pl
from jax.experimental.pallas import tpu as pltpu
from jax.sharding import PartitionSpec as P

LEN = 512
CHUNKS = 4
RAW = 3
FIRST = 4
MESH = pl.DeviceIdType.MESH
VMEM_BYTES = 67_000_000
NT = (((1,), (1,)), ((), ()))
NN = (((1,), (0,)), ((), ()))


def stack_kernel(
    dims,
    owner_ref,
    grad_hbm,
    weight_hbm,
    saved_hbm,
    proj_in_hbm,
    proj_out_hbm,
    query_hbm,
    out_hbm,
    score_hbm,
    raw,
    flat,
    ahead,
    feats,
    part,
    from_left,
    from_right,
    total,
    proj_in,
    proj_out,
    queries,
    saved,
    out_factor,
    in_mine,
    in_peer,
    in_sum,
    run_send,
    run_recv,
    in_total,
    block,
    level_blocks,
    owner_send,
    owner_recv,
    tensor_send,
    tensor_recv,
    seq_blocks,
    flat_blocks,
    score_send,
    score_recv,
    score_total,
    raw_sem,
    io_sem,
    load_sem,
    feat_send,
    feat_recv,
    first_recv,
    part_send,
    left_recv,
    right_recv,
    in_send_sem,
    in_recv_sem,
    run_send_sem,
    run_recv_sem,
    gather_send_sem,
    gather_recv_sem,
    owner_send_sem,
    owner_recv_sem,
    tensor_send_sem,
    tensor_recv_sem,
    seq_send_sem,
    seq_recv_sem,
    score_send_sem,
    score_recv_sem,
):
    layers, n_layer, n_tensor, n_dp, rows, width, rank, step = dims
    last = n_layer - 1
    f32, bf16 = jnp.float32, jnp.bfloat16
    piece_rows = flat.shape[2]
    blocks = piece_rows // step
    per_level = n_layer * blocks
    n_tile = min(512, piece_rows)
    tokens = rows * CHUNKS
    share = tokens // n_tensor
    lanes = 2 * rank
    first_rows = rows // FIRST
    z = lax.axis_index("layer")
    t = lax.axis_index("tensor")
    d = lax.axis_index("dp")

    def nth_piece(i):
        return jnp.where(2 * z < n_layer, last - i, i)

    def raw_copy(n):
        level = layers - 1 - n // per_level
        i = (n // blocks) % n_layer
        start = pl.multiple_of(nth_piece(i) * piece_rows + (n % blocks) * step, step)
        return pltpu.make_async_copy(
            weight_hbm.at[level, pl.ds(start, step)], raw.at[n % RAW], raw_sem.at[n % RAW]
        )

    def relay(first, count):
        @pl.loop(first, first + count)
        def _(n):
            raw_copy(n).wait()

            @pl.when(n + RAW - 1 < layers * per_level)
            def _():
                raw_copy(n + RAW - 1).start()

            level = layers - 1 - n // per_level
            q = nth_piece((n // blocks) % n_layer)
            at = pl.ds(pl.multiple_of((n % blocks) * step, step), step)
            by_feature = jnp.swapaxes(raw[n % RAW], 0, 1)
            for a in range(n_tensor):
                flat[level % 2, q, at, a * width : (a + 1) * width] = by_feature[a]

    def span(c, count=1):
        return pl.ds(pl.multiple_of(c * rows, rows), count * rows)

    def feat_copy(level, c, shift):
        return pltpu.make_async_remote_copy(
            src_ref=feats.at[level % 2, t, span(c)],
            dst_ref=feats.at[level % 2, t, span(c)],
            send_sem=feat_send.at[level % 2, c, shift - 1],
            recv_sem=feat_recv.at[level % 2, c, shift - 1],
            device_id={"tensor": lax.rem(t + shift, n_tensor)},
            device_id_type=MESH,
        )

    def first_copy(half, shift):
        here = slice(half * first_rows, (half + 1) * first_rows)
        return pltpu.make_async_remote_copy(
            src_ref=feats.at[(layers - 1) % 2, t, here],
            dst_ref=feats.at[(layers - 1) % 2, t, here],
            send_sem=feat_send.at[(layers - 1) % 2, 0, shift - 1],
            recv_sem=first_recv.at[half, shift - 1],
            device_id={"tensor": lax.rem(t + shift, n_tensor)},
            device_id_type=MESH,
        )

    def right_copy(slot, level, c, q, first=0, count=rows):
        return pltpu.make_async_remote_copy(
            src_ref=part.at[slot, q, pl.ds(pl.multiple_of((c % 2) * rows + first, count), count)],
            dst_ref=from_left.at[level % 2, c, last - q, first : first + count],
            send_sem=part_send.at[slot, c % 2, q],
            recv_sem=left_recv.at[level % 2, c, last - q],
            device_id={"layer": z + 1},
            device_id_type=MESH,
        )

    def left_copy(slot, level, c, q, first=0, count=rows):
        return pltpu.make_async_remote_copy(
            src_ref=part.at[slot, q, pl.ds(pl.multiple_of((c % 2) * rows + first, count), count)],
            dst_ref=from_right.at[level % 2, c, q, first : first + count],
            send_sem=part_send.at[slot, c % 2, q],
            recv_sem=right_recv.at[level % 2, c, q],
            device_id={"layer": z - 1},
            device_id_type=MESH,
        )

    def wait_part_sends(slot, half):
        for q in range(n_layer):

            if q > 0:

                @pl.when(q > z)
                def _():
                    right_copy(slot, 0, half, q).wait_send()

            if q < last:

                @pl.when(q < z)
                def _():
                    left_copy(slot, 0, half, q).wait_send()

    def send_piece(slot, level, c, q, *part_rows):
        @pl.when((z == 0) & (q > 0))
        def _():
            right_copy(slot, level, c, q, *part_rows).start()

        @pl.when((z == last) & (q < last))
        def _():
            left_copy(slot, level, c, q, *part_rows).start()

    def multiply(slot, level, q, here, there):
        @pl.loop(0, piece_rows // n_tile)
        def _(j):
            at = pl.ds(pl.multiple_of(j * n_tile, n_tile), n_tile)
            acc = None
            for a in range(n_tensor):
                term = lax.dot_general(
                    feats[level % 2, a, here, :],
                    flat[level % 2, q, at, a * width : (a + 1) * width],
                    NT,
                    preferred_element_type=f32,
                )
                acc = term if acc is None else acc + term
            part[slot, q, there, at] = acc.astype(bf16)

    def start_piece(slot, level, q):
        def features_of(a):
            return pl.ds(pl.multiple_of(a * width, width), width)

        @pl.loop(0, piece_rows // n_tile)
        def _(j):
            at = pl.ds(pl.multiple_of(j * n_tile, n_tile), n_tile)
            ahead[:, at] = lax.dot_general(
                feats[level % 2, t, 0:rows, :],
                flat[level % 2, q, at, features_of(t)],
                NT,
                preferred_element_type=f32,
            )

        for k in range(FIRST):
            here = slice(k * first_rows, (k + 1) * first_rows)
            for shift in range(1, n_tensor):
                first_copy(k, shift).wait_recv()

            @pl.loop(0, piece_rows // n_tile)
            def _(j):
                at = pl.ds(pl.multiple_of(j * n_tile, n_tile), n_tile)
                acc = ahead[here, at]
                for shift in range(1, n_tensor):
                    a = lax.rem(t + shift, n_tensor)
                    acc = acc + lax.dot_general(
                        feats[level % 2, a, here, :],
                        flat[level % 2, q, at, features_of(a)],
                        NT,
                        preferred_element_type=f32,
                    )
                part[slot, q, here, at] = acc.astype(bf16)

            send_piece(slot, level, 0, q, k * first_rows, first_rows)
            ready = blocks * k // FIRST
            relay(blocks + ready, blocks * (k + 1) // FIRST - ready)

    def forward(slot, level, c, s):
        right_piece, left_piece = last - s + z, s - last + z

        @pl.when((z > 0) & (right_piece <= last))
        def _():
            right_copy(slot, level, c, right_piece).wait_recv()

            @pl.when(right_piece > z)
            def _():
                part[slot, right_piece, span(c % 2), :] = (
                    part[slot, right_piece, span(c % 2), :].astype(f32)
                    + from_left[level % 2, c, last - right_piece].astype(f32)
                ).astype(bf16)
                right_copy(slot, level, c, right_piece).start()

        @pl.when((z < last) & (left_piece >= 0))
        def _():
            left_copy(slot, level, c, left_piece).wait_recv()

            @pl.when(left_piece < z)
            def _():
                part[slot, left_piece, span(c % 2), :] = (
                    part[slot, left_piece, span(c % 2), :].astype(f32)
                    + from_right[level % 2, c, left_piece].astype(f32)
                ).astype(bf16)
                left_copy(slot, level, c, left_piece).start()

    def grad_copy(c):
        return pltpu.make_async_copy(
            grad_hbm.at[pl.ds(c * rows, rows)], feats.at[(layers - 1) % 2, t, span(c)], io_sem.at[c]
        )

    def out_copy(c):
        return pltpu.make_async_copy(
            feats.at[1, t, span(c)], out_hbm.at[pl.ds(c * rows, rows)], io_sem.at[c]
        )

    def project(level, c):
        out_factor[level, c] = lax.dot_general(
            proj_out[level], feats[level % 2, t, span(c), :], NT, preferred_element_type=f32
        )

    def finish(slot, level, c):
        for shift in range(1, n_tensor):
            feat_copy(level, c, shift).wait_send()
        total[c] = total[c] + part[slot, z, span(c % 2), :].astype(f32)

        @pl.when(z > 0)
        def _():
            total[c] = total[c] + from_left[level % 2, c, last - z].astype(f32)

        @pl.when(z < last)
        def _():
            total[c] = total[c] + from_right[level % 2, c, z].astype(f32)

        feats[(level + 1) % 2, t, span(c), :] = total[c].astype(bf16)

        @pl.when(level > 0)
        def _():
            for shift in range(1, n_tensor):
                feat_copy(level - 1, c, shift).start()
            project(jnp.maximum(level - 1, 0), c)

        @pl.when(level == 0)
        def _():
            out_copy(c).start()

    def begin_total():
        for k in range(CHUNKS):
            total[k] = feats[(layers - 1) % 2, t, span(k), :].astype(f32)
            project(layers - 1, k)

    def saved_copy(level):
        return pltpu.make_async_copy(saved_hbm.at[level], saved, load_sem.at[3])

    def share_of(i):
        return pl.ds(pl.multiple_of(i * share, share), share)

    def in_copy(shift):
        peer = lax.rem(t + shift, n_tensor)
        return pltpu.make_async_remote_copy(
            src_ref=in_mine.at[:, share_of(peer)],
            dst_ref=in_peer.at[shift - 1],
            send_sem=in_send_sem.at[shift - 1],
            recv_sem=in_recv_sem.at[shift - 1],
            device_id={"tensor": peer},
            device_id_type=MESH,
        )

    def run_copy(side):
        return pltpu.make_async_remote_copy(
            src_ref=run_send.at[side],
            dst_ref=run_recv.at[side],
            send_sem=run_send_sem.at[side],
            recv_sem=run_recv_sem.at[side],
            device_id={"layer": z + (1 if side == 0 else -1)},
            device_id_type=MESH,
        )

    def gather_copy(shift):
        return pltpu.make_async_remote_copy(
            src_ref=in_total.at[:, share_of(t)],
            dst_ref=in_total.at[:, share_of(t)],
            send_sem=gather_send_sem.at[shift - 1],
            recv_sem=gather_recv_sem.at[shift - 1],
            device_id={"tensor": lax.rem(t + shift, n_tensor)},
            device_id_type=MESH,
        )

    def owner_copy(shift):
        peer = lax.rem(z + shift, n_layer)
        return pltpu.make_async_remote_copy(
            src_ref=owner_send.at[peer],
            dst_ref=owner_recv.at[shift - 1],
            send_sem=owner_send_sem.at[shift - 1],
            recv_sem=owner_recv_sem.at[shift - 1],
            device_id={"layer": peer},
            device_id_type=MESH,
        )

    def tensor_copy(shift):
        return pltpu.make_async_remote_copy(
            src_ref=tensor_send,
            dst_ref=tensor_recv.at[shift - 1],
            send_sem=tensor_send_sem.at[shift - 1],
            recv_sem=tensor_recv_sem.at[shift - 1],
            device_id={"tensor": lax.rem(t + shift, n_tensor)},
            device_id_type=MESH,
        )

    def seq_copy(shift):
        return pltpu.make_async_remote_copy(
            src_ref=seq_blocks.at[0],
            dst_ref=seq_blocks.at[shift],
            send_sem=seq_send_sem.at[shift - 1],
            recv_sem=seq_recv_sem.at[shift - 1],
            device_id={"dp": lax.rem(d + shift, n_dp)},
            device_id_type=MESH,
        )

    def score_copy(shift):
        peer = lax.rem(z + shift, n_layer)
        return pltpu.make_async_remote_copy(
            src_ref=score_send.at[lax.rem(d - peer + n_dp, n_dp)],
            dst_ref=score_recv.at[shift - 1],
            send_sem=score_send_sem.at[shift - 1],
            recv_sem=score_recv_sem.at[shift - 1],
            device_id={"layer": peer},
            device_id_type=MESH,
        )

    def project_saved(level):
        saved_copy(level).wait()
        pair, half = level // 2, level % 2
        value = lax.dot_general(saved[...], proj_in[pair], NT, preferred_element_type=f32)
        if half == 0:
            in_mine[pair] = value.astype(bf16)
        else:
            lane = lax.broadcasted_iota(jnp.int32, value.shape, 1)
            in_mine[pair] = jnp.where(lane < rank, in_mine[pair].astype(f32), value).astype(bf16)
        if level + 1 < layers:
            saved_copy(level + 1).start()
        else:
            for shift in range(1, n_tensor):
                in_copy(shift).start()

    def run_step(s):
        if s == 0:
            value = in_mine[:, share_of(t)].astype(f32)
            for shift in range(1, n_tensor):
                in_copy(shift).wait()
                value = value + in_peer[shift - 1].astype(f32)
            in_sum[...] = value
        if s < last:

            @pl.when(z == s)
            def _():
                if s > 0:
                    run_copy(0).wait_recv()
                    run_send[0] = (in_sum[...] + run_recv[0].astype(f32)).astype(bf16)
                else:
                    run_send[0] = in_sum[...].astype(bf16)
                run_copy(0).start()

            @pl.when(z == last - s)
            def _():
                if s > 0:
                    run_copy(1).wait_recv()
                    run_send[1] = (in_sum[...] + run_recv[1].astype(f32)).astype(bf16)
                else:
                    run_send[1] = in_sum[...].astype(bf16)
                run_copy(1).start()

        else:

            @pl.when(z == last)
            def _():
                run_copy(0).wait_recv()

            @pl.when(z == 0)
            def _():
                run_copy(1).wait_recv()

            @pl.when(z < last)
            def _():
                run_copy(0).wait_send()
                in_sum[...] = in_sum[...] + run_recv[1].astype(f32)

            @pl.when(z > 0)
            def _():
                run_copy(1).wait_send()
                in_sum[...] = in_sum[...] + run_recv[0].astype(f32)

            in_total[:, share_of(t)] = in_sum[...].astype(bf16)
            for shift in range(1, n_tensor):
                gather_copy(shift).start()

    def send_blocks():
        for shift in range(1, n_tensor):
            gather_copy(shift).wait()
        lane = lax.broadcasted_iota(jnp.int32, (rank // 2, lanes), 1)
        for level in range(layers):
            pair, half = level // 2, level % 2
            acc = None
            for c in range(CHUNKS):
                term = lax.dot_general(
                    out_factor[level, c],
                    in_total[pair, c * rows : (c + 1) * rows].astype(f32),
                    NN,
                    precision=lax.Precision.HIGHEST,
                    preferred_element_type=f32,
                )
                acc = term if acc is None else acc + term
            block[...] = acc
            even = block[pl.ds(0, rank // 2, stride=2), :]
            odd = block[pl.ds(1, rank // 2, stride=2), :]
            if half == 0:
                odd = pltpu.roll(odd, rank, 1)
            else:
                even = pltpu.roll(even, rank, 1)
            level_blocks[level] = jnp.where(lane < rank, even, odd)
        for q in range(n_layer):
            level = jnp.int32(0)
            for k in range(1, layers):
                level = jnp.where(owner_ref[k] == q, k, level)
            owner_send[q] = level_blocks[level]
        for shift in range(1, n_layer):
            owner_copy(shift).start()

    def sum_layers():
        value = owner_send[z]
        for shift in range(1, n_layer):
            owner_copy(shift).wait()
            value = value + owner_recv[shift - 1]
        tensor_send[...] = value
        for shift in range(1, n_tensor):
            tensor_copy(shift).start()

    def sum_tensor():
        value = tensor_send[...]
        for shift in range(1, n_tensor):
            tensor_copy(shift).wait()
            value = value + tensor_recv[shift - 1]
        seq_blocks[0] = value
        for shift in range(1, n_dp):
            seq_copy(shift).start()

    def score():
        for shift in range(1, n_dp):
            seq_copy(shift).wait()
        pltpu.make_async_copy(query_hbm, queries, load_sem.at[2]).wait()
        for j in range(rank // 2):
            flat_blocks[:, j * lanes : (j + 1) * lanes] = seq_blocks[:, j, :]
        acc = lax.dot_general(
            flat_blocks[...].astype(bf16), queries[...], NT, preferred_element_type=f32
        )
        for k in range(n_dp):
            score_send[k] = acc[k : k + 1]
        for shift in range(1, n_layer):
            score_copy(shift).start()

    def score_out():
        return pltpu.make_async_copy(score_total, score_hbm, load_sem.at[4])

    def sum_scores():
        value = score_send[lax.rem(d - z + n_dp, n_dp)]
        for shift in range(1, n_layer):
            score_copy(shift).wait()
            value = value + score_recv[shift - 1]
        score_total[...] = value
        score_out().start()

    barrier = pltpu.get_barrier_semaphore()

    @pl.when(z > 0)
    def _():
        pl.semaphore_signal(barrier, inc=1, device_id={"layer": z - 1}, device_id_type=MESH)

    @pl.when(z < last)
    def _():
        pl.semaphore_signal(barrier, inc=1, device_id={"layer": z + 1}, device_id_type=MESH)

    for axis, size, here in (("tensor", n_tensor, t), ("dp", n_dp, d)):
        for shift in range(1, size):
            pl.semaphore_signal(
                barrier, inc=1, device_id={axis: lax.rem(here + shift, size)}, device_id_type=MESH
            )

    for c in range(CHUNKS):
        grad_copy(c).start()
    for n in range(RAW - 1):
        raw_copy(n).start()
    pltpu.make_async_copy(proj_out_hbm, proj_out, load_sem.at[0]).start()
    pltpu.make_async_copy(proj_in_hbm, proj_in, load_sem.at[1]).start()
    pl.semaphore_wait(
        barrier, n_tensor + n_dp - 2 + jnp.minimum(z, 1) + jnp.minimum(last - z, 1)
    )

    for c in range(CHUNKS):
        grad_copy(c).wait()
        for shift in range(1, n_tensor):
            if c == 0:
                for k in range(FIRST):
                    first_copy(k, shift).start()
            else:
                feat_copy(layers - 1, c, shift).start()

    phases = layers * CHUNKS
    fraction = per_level // (2 * CHUNKS)

    @pl.loop(0, phases - 1)
    def _(p):
        level = layers - 1 - p // CHUNKS
        c = p % CHUNKS
        slot = (p // 2) % 2
        old_level = layers - 1 - (p - 1) // CHUNKS
        old_c = (p + CHUNKS - 1) % CHUNKS
        old_slot = ((p - 1) // 2) % 2

        def at_phase(k, task, *args):
            @pl.when(p == k)
            def _():
                task(*args)

        @pl.when(p > 1)
        def _():
            forward(old_slot, old_level, old_c, 1)

        @pl.when(p == 0)
        def _():
            relay(0, blocks)
            start_piece(slot, level, nth_piece(0))

            @pl.loop(1, n_layer)
            def _(i):
                @pl.when(i > 1)
                def _():
                    relay(i * blocks, blocks)

                multiply(slot, level, nth_piece(i), pl.ds(0, rows), pl.ds(0, rows))
                send_piece(slot, level, 0, nth_piece(i))

            forward(slot, level, 0, 1)

        @pl.when(p == 1)
        def _():
            for shift in range(1, n_tensor):
                feat_copy(level, 1, shift).wait_recv()

            @pl.loop(0, n_layer)
            def _(i):
                multiply(slot, level, nth_piece(i), pl.ds(rows, rows), pl.ds(rows, rows))
                send_piece(slot, level, 1, nth_piece(i))

        @pl.when((p >= 2) & (c % 2 == 0))
        def _():
            @pl.when(p >= 4)
            def _():
                wait_part_sends(slot, 0)
                wait_part_sends(slot, 1)

            for shift in range(1, n_tensor):
                feat_copy(level, c, shift).wait_recv()
                feat_copy(level, c + 1, shift).wait_recv()

            @pl.loop(0, n_layer)
            def _(i):
                q = nth_piece(i)
                multiply(slot, level, q, span(c, 2), pl.ds(0, 2 * rows))

                @pl.when((p < phases - 2) | (i < n_layer - 2))
                def _():
                    send_piece(slot, level, c, q)

                @pl.when((p == phases - 2) & (i < n_layer - 2))
                def _():
                    send_piece(slot, level, c + 1, q)

            @pl.when(p < phases - 2)
            def _():
                for i in range(n_layer):
                    send_piece(slot, level, c + 1, nth_piece(i))

        top = level == layers - 1
        base = (layers - level) * per_level + 2 * fraction * c
        base = jnp.where(top, base - jnp.where(c == CHUNKS - 1, 1, 2) * fraction, base)
        early = jnp.where((c % 2 == 1) & (p > 1), fraction, 0)
        late = jnp.where(top & (c > 1), 3 * fraction, 2 * fraction) - early

        @pl.when(p == 0)
        def _():
            pltpu.make_async_copy(proj_out_hbm, proj_out, load_sem.at[0]).wait()
            pltpu.make_async_copy(proj_in_hbm, proj_in, load_sem.at[1]).wait()
            pltpu.make_async_copy(query_hbm, queries, load_sem.at[2]).start()
            saved_copy(0).start()
        at_phase(phases - 3, send_blocks)

        @pl.when((p > 0) & (level > 0))
        def _():
            relay(base, early)

        for s in range(2, n_layer - 1):

            @pl.when(p > 0)
            def _():
                forward(old_slot, old_level, old_c, s)

        at_phase(1, begin_total)
        for k in range(layers):
            at_phase(CHUNKS + k, project_saved, k)
        for k in range(n_layer):
            at_phase(CHUNKS + layers + 1 + k, run_step, k)

        @pl.when((p > 0) & (level > 0))
        def _():
            relay(base + early, late)

        @pl.when(p > 0)
        def _():
            forward(old_slot, old_level, old_c, last)
            finish(old_slot, old_level, old_c)

    end_slot, end_level = ((phases - 1) // 2) % 2, jnp.int32(0)
    pair = (CHUNKS - 2, CHUNKS - 1)
    def score_and_send():
        score()
        for c in pair:
            send_piece(end_slot, end_level, c, nth_piece(n_layer - 2))

    between = [sum_layers, sum_tensor, score_and_send]
    for s in range(1, last):
        for c in pair:
            forward(end_slot, end_level, c, s)
            if between:
                between.pop(0)()
    for c in pair:
        forward(end_slot, end_level, c, last)
        finish(end_slot, end_level, c)
    sum_scores()
    for k in range(2):
        wait_part_sends(k, 0)
        wait_part_sends(k, 1)
    score_out().wait()
    for c in range(CHUNKS):
        out_copy(c).wait()


def hand_over_kernel(grad_in, score_in, grad_out, score_out, grad, score, in_sem, out_sem):
    count = in_sem.shape[0] - 1
    rows = grad.shape[0] // count

    def copies(source, target, sem):
        for k in range(count):
            at = pl.ds(k * rows, rows)
            yield pltpu.make_async_copy(source[0].at[at], target[0].at[at], sem.at[k])
        yield pltpu.make_async_copy(source[1], target[1], sem.at[count])

    loads = list(copies((grad_in, score_in), (grad, score), in_sem))
    stores = list(copies((grad, score), (grad_out, score_out), out_sem))
    for load in loads:
        load.start()
    for load, store in zip(loads, stores):
        load.wait()
        store.start()
    for store in stores:
        store.wait()


def hand_over(grad, score):
    shapes = tuple(jax.ShapeDtypeStruct(x.shape, x.dtype) for x in (grad, score))
    anywhere = pl.BlockSpec(memory_space=pl.ANY)
    return pl.pallas_call(
        hand_over_kernel,
        out_shape=shapes,
        in_specs=[anywhere] * 2,
        out_specs=(anywhere,) * 2,
        scratch_shapes=[
            pltpu.VMEM(grad.shape, grad.dtype),
            pltpu.VMEM(score.shape, score.dtype),
            pltpu.SemaphoreType.DMA((CHUNKS + 1,)),
            pltpu.SemaphoreType.DMA((CHUNKS + 1,)),
        ],
        name="hand_over",
    )(grad, score)


def on_device(saved_inputs, output_grad, weights, proj_in, proj_out, query_grads, owner_map):
    weights = weights[:, :, :, 0, :]
    layers, in_rows, n_tensor, width = weights.shape
    tokens = output_grad.shape[0]
    rank = proj_out.shape[1]
    n_queries = query_grads.shape[1]
    n_layer, n_dp = lax.axis_size("layer"), lax.axis_size("dp")
    assert tokens == LEN and n_dp == n_layer == layers and layers % 2 == 0
    rows = tokens // CHUNKS
    piece_rows = in_rows // n_layer
    step = min(256, piece_rows // 2)
    pairs, lanes, share = layers // 2, 2 * rank, tokens // n_tensor
    bf16, f32 = jnp.bfloat16, jnp.float32
    dma = pltpu.SemaphoreType.DMA
    hops = n_layer - 1
    anywhere = pl.BlockSpec(memory_space=pl.ANY)
    results = pl.pallas_call(
        functools.partial(
            stack_kernel, (layers, n_layer, n_tensor, n_dp, rows, width, rank, step)
        ),
        out_shape=(
            jax.ShapeDtypeStruct((tokens, width), bf16),
            jax.ShapeDtypeStruct((1, n_queries), f32),
        ),
        in_specs=[pl.BlockSpec(memory_space=pltpu.SMEM)] + [anywhere] * 6,
        out_specs=(anywhere, anywhere),
        scratch_shapes=[
            pltpu.VMEM((RAW, step, n_tensor, width), bf16),
            pltpu.VMEM((2, n_layer, piece_rows, n_tensor * width), bf16),
            pltpu.VMEM((rows, piece_rows), f32),
            pltpu.VMEM((2, n_tensor, tokens, width), bf16),
            pltpu.VMEM((2, n_layer, 2 * rows, piece_rows), bf16),
            pltpu.VMEM((2, CHUNKS, hops, rows, piece_rows), bf16),
            pltpu.VMEM((2, CHUNKS, hops, rows, piece_rows), bf16),
            pltpu.VMEM((CHUNKS, rows, width), f32),
            pltpu.VMEM((pairs, lanes, width), bf16),
            pltpu.VMEM((layers, rank, width), bf16),
            pltpu.VMEM(query_grads.shape[1:], bf16),
            pltpu.VMEM((tokens, width), bf16),
            pltpu.VMEM((layers, CHUNKS, rank, rows), f32),
            pltpu.VMEM((pairs, tokens, lanes), bf16),
            pltpu.VMEM((n_tensor - 1, pairs, share, lanes), bf16),
            pltpu.VMEM((pairs, share, lanes), f32),
            pltpu.VMEM((2, pairs, share, lanes), bf16),
            pltpu.VMEM((2, pairs, share, lanes), bf16),
            pltpu.VMEM((pairs, tokens, lanes), bf16),
            pltpu.VMEM((rank, lanes), f32),
            pltpu.VMEM((layers, rank // 2, lanes), f32),
            pltpu.VMEM((n_layer, rank // 2, lanes), f32),
            pltpu.VMEM((hops, rank // 2, lanes), f32),
            pltpu.VMEM((rank // 2, lanes), f32),
            pltpu.VMEM((n_tensor - 1, rank // 2, lanes), f32),
            pltpu.VMEM((n_dp, rank // 2, lanes), f32),
            pltpu.VMEM((n_dp, rank * rank), f32),
            pltpu.VMEM((n_dp, 1, n_queries), f32),
            pltpu.VMEM((hops, 1, n_queries), f32),
            pltpu.VMEM((1, n_queries), f32),
            dma((RAW,)),
            dma((CHUNKS,)),
            dma((5,)),
            dma((2, CHUNKS, n_tensor - 1)),
            dma((2, CHUNKS, n_tensor - 1)),
            dma((FIRST, n_tensor - 1)),
            dma((2, 2, n_layer)),
            dma((2, CHUNKS, hops)),
            dma((2, CHUNKS, hops)),
            dma((n_tensor - 1,)),
            dma((n_tensor - 1,)),
            dma((2,)),
            dma((2,)),
            dma((n_tensor - 1,)),
            dma((n_tensor - 1,)),
            dma((hops,)),
            dma((hops,)),
            dma((n_tensor - 1,)),
            dma((n_tensor - 1,)),
            dma((n_dp - 1,)),
            dma((n_dp - 1,)),
            dma((hops,)),
            dma((hops,)),
        ],
        compiler_params=pltpu.CompilerParams(
            collective_id=0, has_side_effects=True, vmem_limit_bytes=VMEM_BYTES
        ),
        name="backward_stack",
    )(
        owner_map,
        output_grad,
        weights,
        saved_inputs,
        proj_in.reshape(pairs, lanes, width),
        proj_out,
        query_grads[0],
    )
    return hand_over(*results)


def solution(mesh):
    in_specs = (
        P(None, "dp", ("tensor", "layer")),
        P("dp", ("tensor", "layer")),
        P(None, "tensor", None, "layer", None),
        P(None, None, ("tensor", "layer")),
        P(None, None, ("tensor", "layer")),
        P("layer", ("dp", "tensor"), None),
        P(),
    )
    out_specs = (P("dp", ("tensor", "layer")), P("layer", ("dp", "tensor")))
    return jax.shard_map(
        on_device, mesh=mesh, in_specs=in_specs, out_specs=out_specs, check_vma=False
    )
```
